512 devices in a mesh: dp: 128 (over z, y, core), tensor: 4 (over x).
Axes of the slice: x: 4, y: 4, z: 16, core: 2. Of those that a mesh axis runs over, the one named last changes fastest.
Arguments:
- patches: bfloat16 [131072, 1280], P('dp', 'tensor'), may hold values from -60 to 60
- counts: int32 [256], replicated, may hold values from 0 to 512, as said below
- first_gain: float32 [1280], replicated, may hold values from 0.1 to 1.9
- first_shift: float32 [1280], replicated, may hold values from -3 to 3
- in_weight: bfloat16 [1280, 3, 1280], P(None, None, 'tensor'), may hold values from -0.15625 to 0.15625
- in_bias: float32 [3, 1280], P(None, 'tensor'), may hold values from -30 to 30
- out_weight: bfloat16 [1280, 1280], P(None, 'tensor'), may hold values from -0.15625 to 0.15625
- out_bias: float32 [1280], P('tensor'), may hold values from -3 to 3
- second_gain: float32 [1280], P('tensor'), may hold values from 0.1 to 1.9
- second_shift: float32 [1280], P('tensor'), may hold values from -3 to 3
- merger_weight: bfloat16 [4, 1280, 4096], P(None, 'tensor', 'dp'), may hold values from -0.078125 to 0.078125
- merger_bias: float32 [4096], replicated, may hold values from -4 to 4
Outputs:
- embeds: bfloat16 [32768, 4096], P(('dp', 'tensor'))
The draws below stay inside these ranges and needn't reach their ends.
Inputs may be any that keep to these rules, and one draw needn't show every extreme that they name: Entry 2 r + j is the patch count of slot j of data rank r, 0 for an empty slot; a rank's images fill its slots from slot 0; counts are multiples of 4; ranks 2 i and 2 i + 1 hold at most two images together, and in every draw some rank holds two.
All inputs are finite; a program needn't handle non-finite values.
Results may differ from the reference program's by a relative error of at most 0.0095.
Values may be sent and summed in bfloat16 or wider, within the bound.
A program may use at most 128 MiB of HBM per device.

```python
import math
import jax
import jax.numpy as jnp
from jax import lax

D = 1280
HEADS = 16
LLMW = 4096
TILE = 512
IMAGE_SLOTS = 256
ROWS = 32768
N_TENSOR = 4


def draw_patches(key, part):
    first = jax.random.fold_in(jax.random.fold_in(key, 11), 0)
    base = jax.random.normal(first, (IMAGE_SLOTS * TILE, D), jnp.float32)
    return jnp.clip(base, -60.0, 60.0).astype(jnp.bfloat16)


def draw_in_bias(key, part):
    first = jax.random.fold_in(jax.random.fold_in(key, 23), 0)
    base = 0.5 * jax.random.normal(first, (3, D), jnp.float32)
    return jnp.clip(base, -30.0, 30.0)


def draw_counts(key, part):
    first, second, third = jax.random.split(jax.random.fold_in(key, 37), 3)
    pairs = IMAGE_SLOTS // 4
    pattern = jax.random.randint(first, (pairs,), 0, 6)
    forced = jax.random.randint(second, (), 0, 2)
    pattern = jnp.where(jnp.arange(pairs) == 0, forced, pattern)
    table_left = jnp.array([2, 0, 1, 1, 0, 0], jnp.int32)
    table_right = jnp.array([0, 2, 1, 0, 1, 0], jnp.int32)
    left = table_left[pattern]
    right = table_right[pattern]
    sizes = jax.random.randint(third, (pairs, 4), TILE // 8, TILE // 4 + 1) * 4
    first_cell = (jnp.arange(pairs)[:, None] == 0) & (jnp.arange(4)[None, :] == 0)
    sizes = jnp.where(first_cell, TILE, sizes)
    slot_number = jnp.array([0, 1, 0, 1], jnp.int32)[None, :]
    holder = jnp.where(jnp.array([True, True, False, False])[None, :], left[:, None], right[:, None])
    live = slot_number < holder
    return jnp.where(live, sizes, 0).reshape(IMAGE_SLOTS).astype(jnp.int32)


def shard_levels(rng, shape, shards, least, high):
    def one(position, parts):
        heights = jax.random.uniform(jax.random.fold_in(jax.random.fold_in(rng, 6), position), (parts,), jnp.float32, least / len(shards), high / len(shards))
        return jnp.repeat(jnp.exp(heights), shape[position] // parts).reshape((-1,) + (1,) * (len(shape) - position - 1))

    loudness = one(*shards[0])
    for cut in shards[1:]:
        loudness = loudness * one(*cut)
    return loudness


def gaussian(key, shape, deviation, bound, pieces=(), kind=jnp.bfloat16):
    values = jax.random.normal(key, shape, jnp.float32) * deviation
    if len(pieces) > 0:
        values = shard_levels(key, shape, pieces, -0.22, 0.18) * values
    return jnp.clip(values, min=-bound, max=bound).astype(kind)


def setup_inputs(seed: int = 0) -> dict:
    streams_of = jax.random.split(jax.random.key(seed), 13)
    return {
        "patches": draw_patches(jax.random.fold_in(streams_of[12], 71), 0),
        "counts": draw_counts(jax.random.fold_in(streams_of[12], 71), 0),
        "first_gain": jnp.clip(1.0 + 0.18 * jax.random.normal(streams_of[2], (D,), jnp.float32), 0.1, 1.9),
        "first_shift": gaussian(streams_of[3], (D,), 0.5, 3.0, (), jnp.float32),
        "in_weight": gaussian(streams_of[4], (D, 3, D), D ** -0.5, 0.15625, ((2, 4),)),
        "in_bias": draw_in_bias(jax.random.fold_in(streams_of[12], 71), 0),
        "out_weight": gaussian(streams_of[6], (D, D), D ** -0.5, 0.15625, ((1, 4),)),
        "out_bias": gaussian(streams_of[7], (D,), 0.5, 3.0, ((0, 4),), jnp.float32),
        "second_gain": jnp.clip(1.0 + 0.18 * jax.random.normal(streams_of[8], (D,), jnp.float32), 0.1, 1.9),
        "second_shift": gaussian(streams_of[9], (D,), 0.5, 3.0, ((0, 4),), jnp.float32),
        "merger_weight": gaussian(streams_of[10], (4, D, LLMW), (4 * D) ** -0.5, 0.078125, ((1, 4), (2, 128))),
        "merger_bias": gaussian(streams_of[11], (LLMW,), 1.0, 4.0, (), jnp.float32),
    }


EPS = 1e-06
MASKED = -1e+30

def layer_norm(values, gain, shift):
    row_mean = lax.optimization_barrier(jnp.mean(values, axis=-1, keepdims=True))
    centred = values - row_mean
    spread = lax.optimization_barrier(jnp.mean(centred * centred, axis=-1, keepdims=True))
    return centred * lax.rsqrt(spread + EPS) * gain + shift

def reference(patches, counts, first_gain, first_shift, in_weight, in_bias, out_weight, out_bias, second_gain, second_shift, merger_weight, merger_bias):
    head_size = D // HEADS
    scale = 1.0 / math.sqrt(head_size)
    block = D // N_TENSOR
    slot_view = patches.reshape(IMAGE_SLOTS, TILE, D)
    positions = jnp.arange(TILE, dtype=jnp.int32)
    merged_index = jnp.arange(TILE // 4, dtype=jnp.int32)

    def encode_slot(operand):
        tile, count = operand
        values = tile.astype(jnp.float32)
        normed = layer_norm(values, first_gain, first_shift).astype(jnp.bfloat16)
        projected = jnp.dot(normed, in_weight.reshape(D, 3 * D), preferred_element_type=jnp.float32) + in_bias.reshape(3 * D)
        projected = projected.astype(jnp.bfloat16).reshape(TILE, 3, HEADS, head_size).astype(jnp.float32)
        scores = jnp.einsum('qhd,khd->hqk', projected[:, 0], projected[:, 1]) * scale
        scores = jnp.where((positions < count)[None, None, :], scores, MASKED)
        highest = lax.optimization_barrier(jnp.max(scores, axis=-1, keepdims=True))
        raised = jnp.exp(scores - highest)
        weights = (raised / lax.optimization_barrier(jnp.sum(raised, axis=-1, keepdims=True))).astype(jnp.bfloat16)
        heads_out = jnp.einsum('hqk,khd->qhd', weights.astype(jnp.float32), projected[:, 2])
        heads_out = heads_out.astype(jnp.bfloat16).reshape(TILE, D)
        residual = values + jnp.dot(heads_out, out_weight, preferred_element_type=jnp.float32) + out_bias
        row_mean = lax.optimization_barrier(jnp.sum(residual, axis=1, keepdims=True)) / D
        second = lax.optimization_barrier(jnp.sum(residual * residual, axis=1, keepdims=True)) / D
        encoded = (residual - row_mean) * lax.rsqrt(second - row_mean * row_mean + EPS) * second_gain + second_shift
        merged = encoded.astype(jnp.bfloat16).reshape(TILE // 4, 4, D)
        total = jnp.zeros((TILE // 4, LLMW), jnp.float32)
        for feature_block in range(N_TENSOR):
            lower = feature_block * block
            piece = merged[:, :, lower:lower + block].reshape(TILE // 4, 4 * block)
            rows = merger_weight[:, lower:lower + block, :].reshape(4 * block, LLMW)
            partial_value = jnp.dot(piece, rows, preferred_element_type=jnp.float32).astype(jnp.bfloat16)
            total = total + lax.optimization_barrier(partial_value).astype(jnp.float32)
        embedded = total + merger_bias
        keep = (merged_index * 4 < count)[:, None]
        return jnp.where(keep, embedded, 0.0).astype(jnp.bfloat16)

    def empty_slot(operand):
        return jnp.zeros((TILE // 4, LLMW), jnp.bfloat16)

    def one_slot(operand):
        return lax.cond(operand[1] > 0, encode_slot, empty_slot, operand)
    result = lax.map(one_slot, (slot_view, counts))
    return result.reshape(ROWS, LLMW)
```

```python
import functools
import math

import jax
import jax.numpy as jnp
from jax import lax
from jax.experimental import pallas as pl
from jax.experimental.pallas import tpu as pltpu
from jax.sharding import PartitionSpec as P

D = 1280
HEADS = 16
TILE = 512
NX = 4
NY = 4
NZ = 16
BLOCK = D // NX
HEAD = D // HEADS
LOCAL_HEADS = BLOCK // HEAD
LLMW = 4096
MROWS = TILE // 4
HALF = MROWS // 2
QUARTER = HALF // 2
ZCOLS = LLMW // NZ
PHASES = NZ // 2

EPS = 1e-06
MASKED = -1e30
MESH = pl.DeviceIdType.MESH
F32 = jnp.float32
BF16 = jnp.bfloat16
CHUNK = 80

NT = (((1,), (1,)), ((), ()))
TN = (((0,), (0,)), ((), ()))


def kernel(
    counts,
    patches,
    in_w_hbm,
    out_w_hbm,
    vec,
    mw,
    mbias,
    out,
    slot0,
    slot1,
    xbuf,
    hbuf,
    in_w,
    out_w,
    vt,
    normed,
    proj,
    stat,
    resid,
    wbuf,
    merged,
    pbuf,
    xpb,
    rel_a,
    rel_b,
    rs_a,
    rs_b,
    fa1,
    fa2,
    fb1,
    fb2,
    local_sem,
    part_send,
    part_recv,
    g_send,
    g_recv,
    h_send,
    h_recv,
    st_send,
    st_recv,
    y_send,
    y_recv,
    up_send,
    up_recv,
    dn_send,
    dn_recv,
    pf_send,
    pf_recv,
    rs_send,
    rs_recv,
):
    rank = lax.axis_index("dp")
    t = lax.axis_index("tensor")
    c = lax.rem(rank, 2)
    y = lax.rem(rank // 2, NY)
    z = rank // (2 * NY)
    partner = rank + 1 - 2 * c
    right = lax.rem(t + 1, NX)
    left = lax.rem(t + NX - 1, NX)
    across = lax.rem(t + 2, NX)

    def zwrap(k):
        return lax.rem(k + NZ, NZ)

    def rank_of(zz, yy):
        return (zz * NY + yy) * 2 + c

    up = rank_of(zwrap(z + 1), y)
    down = rank_of(zwrap(z - 1), y)

    peers = [(rank, right), (rank, left), (partner, right), (partner, left), (rank, across), (partner, t)]
    peers += [(rank_of(z, lax.rem(y + dy, NY)), t) for dy in range(1, NY)]
    peers += [(up, t), (down, t)]
    barrier = pltpu.get_barrier_semaphore()
    for peer in peers:
        pl.semaphore_signal(barrier, inc=1, device_id=peer, device_id_type=MESH)
    pl.semaphore_wait(barrier, len(peers))

    def remote(src, dst, send, recv, device):
        return pltpu.make_async_remote_copy(
            src_ref=src, dst_ref=dst, send_sem=send, recv_sem=recv, device_id=device, device_id_type=MESH
        )

    swap = remote(patches.at[:, pl.ds(TILE, TILE)], slot1, part_send, part_recv, (partner, t))
    swap.start()
    first = pltpu.make_async_copy(patches.at[:, pl.ds(0, TILE)], slot0, local_sem.at[0])
    first.start()
    mine = pltpu.make_async_copy(mw, wbuf.at[z, y, c], local_sem.at[1])
    mine.start()
    y_copies = []
    for dy in range(1, NY):
        copy = remote(
            mw,
            wbuf.at[z, y, c],
            y_send.at[dy - 1],
            y_recv.at[dy - 1],
            (rank_of(z, lax.rem(y + dy, NY)), t),
        )
        copy.start()
        y_copies.append(copy)
    win_copy = pltpu.make_async_copy(in_w_hbm, in_w, local_sem.at[2])
    win_copy.start()
    wout_copy = pltpu.make_async_copy(out_w_hbm, out_w, local_sem.at[3])
    wout_copy.start()
    vt[...] = jnp.transpose(vec[...])

    def sub(buf, owner, h):
        return buf.at[pl.ds(pl.multiple_of(owner * BLOCK + h * HEAD, 16), HEAD)]

    def gather_copy(buf, send, recv, owner, h, way, hop):
        ref = sub(buf, owner, h)
        return remote(ref, ref, send.at[way, hop, h], recv.at[way, hop, h], (rank, right if way == 0 else left))

    def gather_wait(buf, send, recv, h, way, hop):
        owner = lax.rem(t + (NX - 1 - hop if way == 0 else 1 + hop), NX)
        ref = sub(buf, owner, h)
        remote(ref, ref, send.at[way, hop, h], recv.at[way, hop, h], (rank, right)).wait_recv()

    def own_send(buf, send, recv, h, way):
        gather_copy(buf, send, recv, t, h, way, 0).start()

    def forward(buf, send, recv, h):
        way = h % 2
        gather_wait(buf, send, recv, h, way, 0)
        owner = left if way == 0 else right
        gather_copy(buf, send, recv, owner, h, way, 1).start()

    def finish_gather(buf, send, recv):
        for h in range(LOCAL_HEADS):
            gather_wait(buf, send, recv, h, 1 - h % 2, 0)
        for h in range(LOCAL_HEADS):
            gather_wait(buf, send, recv, h, h % 2, 1)

    def drain_gather(buf, send, recv):
        for h in range(LOCAL_HEADS):
            for way in range(2):
                gather_copy(buf, send, recv, t, h, way, 0).wait_send()
            gather_copy(buf, send, recv, t, h, h % 2, 1).wait_send()

    def zblock(zz):
        return wbuf.at[zz, :, c]

    def up_copy(s):
        ref = zblock(zwrap(z - (s - 1)))
        return remote(ref, ref, up_send.at[s - 1], up_recv.at[s - 1], (up, t))

    def down_copy(s):
        ref = zblock(zwrap(z + (s - 1)))
        return remote(ref, ref, dn_send.at[s - 1], dn_recv.at[s - 1], (down, t))

    def hand_over(index, zz):
        ref = zblock(zz)
        return remote(ref, ref, pf_send.at[index], pf_recv.at[index], (partner, t))

    def hand_wait(index, zz):
        ref = wbuf.at[zz, :, 1 - c]
        remote(ref, ref, pf_send.at[index], pf_recv.at[index], (partner, t)).wait_recv()

    def weights_begin():
        mine.wait()
        for dy in range(1, NY):
            ref = wbuf.at[z, lax.rem(y + NY - dy, NY), c]
            remote(ref, ref, y_send.at[dy - 1], y_recv.at[dy - 1], (rank, t)).wait_recv()
        up_copy(1).start()
        down_copy(1).start()
        hand_over(0, z).start()

    def weights_step(s):
        from_below, from_above = zwrap(z - s), zwrap(z + s)
        ref = zblock(from_below)
        remote(ref, ref, up_send.at[s - 1], up_recv.at[s - 1], (up, t)).wait_recv()
        if s + 1 <= PHASES:
            up_copy(s + 1).start()
        if s < PHASES:
            ref = zblock(from_above)
            remote(ref, ref, dn_send.at[s - 1], dn_recv.at[s - 1], (down, t)).wait_recv()
            if s + 1 < PHASES:
                down_copy(s + 1).start()
        hand_over(2 * s - 1, from_below).start()
        if s < PHASES:
            hand_over(2 * s, from_above).start()

    own0 = counts[2 * rank]
    other1 = counts[2 * partner + 1]
    tile_count = jnp.where(own0 > 0, own0, other1)
    first.wait()
    swap.wait_recv()

    def choose(i, carry):
        rows = pl.ds(pl.multiple_of(i * CHUNK, 16), CHUNK)
        pick = jnp.full((CHUNK, TILE), own0, jnp.int32) > 0
        value = jnp.where(pick, slot0[rows, :].astype(F32), slot1[rows, :].astype(F32))
        xbuf[pl.ds(pl.multiple_of(t * BLOCK + i * CHUNK, 16), CHUNK), :] = value.astype(BF16)
        return carry

    lax.fori_loop(0, BLOCK // CHUNK, choose, 0)
    for h in (0, 2, 1, 3):
        own_send(xbuf, g_send, g_recv, h, 0)
        own_send(xbuf, g_send, g_recv, (h + 1) if h % 2 == 0 else (h - 1), 1)
    weights_begin()
    for h in range(LOCAL_HEADS):
        forward(xbuf, g_send, g_recv, h)
    finish_gather(xbuf, g_send, g_recv)
    weights_step(1)

    def total_of(i, acc):
        x = xbuf[pl.ds(pl.multiple_of(i * CHUNK, 16), CHUNK), :].astype(F32)
        return acc + jnp.sum(x, axis=0, keepdims=True)

    zero_row = jnp.zeros((1, TILE), F32)
    mean = lax.fori_loop(0, D // CHUNK, total_of, zero_row) * (1.0 / D)

    def spread_of(i, acc):
        x = xbuf[pl.ds(pl.multiple_of(i * CHUNK, 16), CHUNK), :].astype(F32) - mean
        return acc + jnp.sum(x * x, axis=0, keepdims=True)

    spread = lax.fori_loop(0, D // CHUNK, spread_of, zero_row) * (1.0 / D)
    inv = lax.rsqrt(spread + EPS)

    def normalise(i, carry):
        rows = pl.ds(pl.multiple_of(i * CHUNK, 16), CHUNK)
        x = xbuf[rows, :].astype(F32)
        gain = vt[rows, 0:1]
        shift = vt[rows, 1:2]
        normed[rows, :] = ((x - mean) * inv * gain + shift).astype(BF16)
        return carry

    lax.fori_loop(0, D // CHUNK, normalise, 0)

    win_copy.wait()
    for part in range(3):
        rows = pl.ds(part * BLOCK, BLOCK)
        got = jnp.dot(in_w[rows, :], normed[...], preferred_element_type=F32)
        proj[rows, :] = (got + vt[rows, 2:3]).astype(BF16)
    weights_step(2)

    scale = 1.0 / math.sqrt(HEAD)

    def attend(h):
        q_rows = pl.ds(h * HEAD, HEAD)
        k_rows = pl.ds(BLOCK + h * HEAD, HEAD)
        v_rows = pl.ds(2 * BLOCK + h * HEAD, HEAD)
        live = lax.broadcasted_iota(jnp.int32, (TILE, TILE // 2), 0) < tile_count

        def columns(i, carry):
            cols = pl.ds(pl.multiple_of(i * (TILE // 2), 128), TILE // 2)
            scores = lax.dot_general(proj[k_rows, :], proj[q_rows, cols], TN, preferred_element_type=F32)
            scores = jnp.where(live, scores * scale, MASKED)
            highest = jnp.max(scores, axis=0, keepdims=True)
            raised = jnp.exp(scores - highest)
            weights = (raised * (1.0 / jnp.sum(raised, axis=0, keepdims=True))).astype(BF16)
            got = jnp.dot(proj[v_rows, :], weights, preferred_element_type=F32)
            hbuf[pl.ds(pl.multiple_of(t * BLOCK + h * HEAD, 16), HEAD), cols] = got.astype(BF16)
            return carry

        lax.fori_loop(0, 2, columns, 0)

    for h in range(LOCAL_HEADS):
        attend(h)
        own_send(hbuf, h_send, h_recv, h, 0)
        own_send(hbuf, h_send, h_recv, h, 1)
        if h >= 2:
            forward(hbuf, h_send, h_recv, h - 2)
    forward(hbuf, h_send, h_recv, 2)
    forward(hbuf, h_send, h_recv, 3)
    weights_step(3)
    finish_gather(hbuf, h_send, h_recv)

    wout_copy.wait()
    got = jnp.dot(out_w[...], hbuf[...], preferred_element_type=F32)
    resid[...] = xbuf[pl.ds(pl.multiple_of(t * BLOCK, 16), BLOCK), :].astype(F32) + got + vt[0:BLOCK, 3:4]

    def sums_of(i, acc):
        x = resid[pl.ds(pl.multiple_of(i * CHUNK, 16), CHUNK), :]
        return acc[0] + jnp.sum(x, axis=0, keepdims=True), acc[1] + jnp.sum(x * x, axis=0, keepdims=True)

    row_sum, row_squares = lax.fori_loop(0, BLOCK // CHUNK, sums_of, (zero_row, zero_row))
    stat[3] = jnp.concatenate([row_sum, row_squares, jnp.zeros((6, TILE), F32)], axis=0)
    targets = (right, left, across)
    for k in range(3):
        remote(stat.at[3], stat.at[k], st_send.at[k], st_recv.at[k], (rank, targets[k])).start()
    weights_step(4)
    for k in range(3):
        remote(stat.at[3], stat.at[k], st_send.at[k], st_recv.at[k], (rank, targets[k])).wait_recv()
    sums = stat[0] + stat[1] + stat[2] + stat[3]
    row_mean = sums[0:1] * (1.0 / D)
    second = sums[1:2] * (1.0 / D)
    inv2 = lax.rsqrt(second - row_mean * row_mean + EPS)

    def encode(i, carry):
        rows = pl.ds(pl.multiple_of(i * CHUNK, 16), CHUNK)
        x = resid[rows, :]
        value = (x - row_mean) * inv2 * vt[rows, 4:5] + vt[rows, 5:6]
        proj[rows, :] = value.astype(BF16)
        return carry

    lax.fori_loop(0, BLOCK // CHUNK, encode, 0)
    pieces = []
    for j in range(4):
        chosen = (
            lax.broadcasted_iota(jnp.int32, (MROWS, TILE), 1)
            == 4 * lax.broadcasted_iota(jnp.int32, (MROWS, TILE), 0) + j
        )
        pick = jnp.where(chosen, 1.0, 0.0).astype(BF16)
        pieces.append(lax.dot_general(pick, proj[0:BLOCK, :], NT, preferred_element_type=F32))
    merged[...] = jnp.concatenate(pieces, axis=1).astype(BF16)

    same = pl.multiple_of(lax.rem(t, 2) * HALF, 16)
    other = pl.multiple_of(HALF - lax.rem(t, 2) * HALF, 16)
    upper = t // 2
    right_up, left_up = right // 2, left // 2
    right_rank = rank + (partner - rank) * right_up
    left_rank = rank + (partner - rank) * left_up

    def rs_copies(s):
        a_same, b_same = pl.ds(same, QUARTER), pl.ds(pl.multiple_of(same + QUARTER, 16), QUARTER)
        a_other, b_other = pl.ds(other, QUARTER), pl.ds(pl.multiple_of(other + QUARTER, 16), QUARTER)
        return (
            remote(pbuf.at[s, a_same], rel_a.at[s], rs_send.at[s, 0], rs_recv.at[s, 0], (rank, right)),
            remote(pbuf.at[s, b_same], rel_b.at[s], rs_send.at[s, 1], rs_recv.at[s, 1], (rank, left)),
            remote(pbuf.at[s, b_other], fb1.at[s], rs_send.at[s, 2], rs_recv.at[s, 2], (right_rank, right)),
            remote(pbuf.at[s, a_other], fa1.at[s], rs_send.at[s, 3], rs_recv.at[s, 3], (left_rank, left)),
            remote(rs_a.at[s], fa2.at[s], rs_send.at[s, 4], rs_recv.at[s, 4], (right_rank, right)),
            remote(rs_b.at[s], fb2.at[s], rs_send.at[s, 5], rs_recv.at[s, 5], (left_rank, left)),
            remote(pbuf.at[s, pl.ds(same, HALF)], xpb.at[s], rs_send.at[s, 6], rs_recv.at[s, 6], (partner, t)),
        )

    def z_of(s):
        return (zwrap(z - s), zwrap(z + s)) if s else (z, zwrap(z - PHASES))

    def project(s):
        for k, zz in enumerate(z_of(s)):
            part = wbuf[zz].reshape(ZCOLS, D)
            got = lax.dot_general(merged[...], part, NT, preferred_element_type=F32)
            pbuf[s, :, k * ZCOLS : (k + 1) * ZCOLS] = got.astype(BF16)
        copies = rs_copies(s)
        for k in (0, 1, 2, 3, 6):
            copies[k].start()

    def relay(s):
        copies = rs_copies(s)
        copies[0].wait_recv()
        own = pbuf[s, pl.ds(other, QUARTER), :].astype(F32)
        rs_a[s] = (rel_a[s].astype(F32) + own).astype(BF16)
        copies[4].start()
        copies[1].wait_recv()
        own = pbuf[s, pl.ds(pl.multiple_of(other + QUARTER, 16), QUARTER), :].astype(F32)
        rs_b[s] = (rel_b[s].astype(F32) + own).astype(BF16)
        copies[5].start()

    my_count = counts[2 * rank + upper]

    def collect(s):
        copies = rs_copies(s)
        for k in (2, 3, 4, 5, 6):
            copies[k].wait_recv()
        local = pbuf[s, pl.ds(same, HALF), :].astype(F32)
        passed = xpb[s].astype(F32)
        is_upper = jnp.full((HALF, 2 * ZCOLS), upper, jnp.int32) > 0
        total = jnp.where(is_upper, passed, local)
        top = fa1[s].astype(F32) + fa2[s].astype(F32)
        bottom = fb1[s].astype(F32) + fb2[s].astype(F32)
        total = total + jnp.concatenate([top, bottom], axis=0)
        row = lax.broadcasted_iota(jnp.int32, (HALF, ZCOLS), 0) + lax.rem(t, 2) * HALF
        keep = 4 * row < my_count
        for k, zz in enumerate(z_of(s)):
            cols = pl.ds(pl.multiple_of(zz * ZCOLS, 128), ZCOLS)
            value = total[:, k * ZCOLS : (k + 1) * ZCOLS] + mbias[:, cols]
            out[:, cols] = jnp.where(keep, value, 0.0).astype(BF16)

    hand_wait(0, z)
    order = (1, 2, 3, 4, 5, 6, 7, 0)
    for n, s in enumerate(order):
        if n + 5 <= PHASES:
            if n >= 1 or True:
                weights_step(n + 5)
        if s:
            hand_wait(2 * s - 1, zwrap(z - s))
            hand_wait(2 * s, zwrap(z + s))
        else:
            hand_wait(2 * PHASES - 1, zwrap(z - PHASES))
        project(s)
        if n >= 1:
            relay(order[n - 1])
        if n >= 3:
            collect(order[n - 3])
    relay(order[7])
    for n in (5, 6, 7):
        collect(order[n])

    swap.wait_send()
    for copy in y_copies:
        copy.wait_send()
    drain_gather(xbuf, g_send, g_recv)
    drain_gather(hbuf, h_send, h_recv)
    for k in range(3):
        remote(stat.at[3], stat.at[k], st_send.at[k], st_recv.at[k], (rank, targets[k])).wait_send()
    for s in range(1, PHASES + 1):
        up_copy(s).wait_send()
        if s < PHASES:
            down_copy(s).wait_send()
    for index in range(NZ):
        hand_over(index, z).wait_send()
    for s in range(PHASES):
        for copy in rs_copies(s):
            copy.wait_send()


def per_device(
    patches,
    counts,
    first_gain,
    first_shift,
    in_weight,
    in_bias,
    out_weight,
    out_bias,
    second_gain,
    second_shift,
    merger_weight,
    merger_bias,
):
    def padded(v):
        return jnp.pad(v.reshape(-1), (0, D - v.size))

    zero = jnp.zeros((D,), F32)
    vec = jnp.stack(
        [first_gain, first_shift, padded(in_bias), padded(out_bias), padded(second_gain), padded(second_shift), zero, zero]
    )
    mw = jnp.transpose(merger_weight, (2, 0, 1)).reshape(LLMW // 128, D)
    any_spec = pl.BlockSpec(memory_space=pl.ANY)
    vmem = pl.BlockSpec(memory_space=pltpu.VMEM)
    dma = pltpu.SemaphoreType.DMA
    return pl.pallas_call(
        kernel,
        out_shape=jax.ShapeDtypeStruct((HALF, LLMW), BF16),
        in_specs=[pl.BlockSpec(memory_space=pltpu.SMEM), any_spec, any_spec, any_spec, vmem, any_spec, vmem],
        out_specs=vmem,
        scratch_shapes=[
            pltpu.VMEM((BLOCK, TILE), BF16),
            pltpu.VMEM((BLOCK, TILE), BF16),
            pltpu.VMEM((D, TILE), BF16),
            pltpu.VMEM((D, TILE), BF16),
            pltpu.VMEM((3 * BLOCK, D), BF16),
            pltpu.VMEM((BLOCK, D), BF16),
            pltpu.VMEM((D, 8), F32),
            pltpu.VMEM((D, TILE), BF16),
            pltpu.VMEM((3 * BLOCK, TILE), BF16),
            pltpu.VMEM((4, 8, TILE), F32),
            pltpu.VMEM((BLOCK, TILE), F32),
            pltpu.VMEM((NZ, NY, 2, 32, D), BF16),
            pltpu.VMEM((MROWS, D), BF16),
            pltpu.VMEM((PHASES, MROWS, 2 * ZCOLS), BF16),
            pltpu.VMEM((PHASES, HALF, 2 * ZCOLS), BF16),
        ]
        + [pltpu.VMEM((PHASES, QUARTER, 2 * ZCOLS), BF16)] * 8
        + [
            dma((4,)),
            dma,
            dma,
            dma((2, 2, LOCAL_HEADS)),
            dma((2, 2, LOCAL_HEADS)),
            dma((2, 2, LOCAL_HEADS)),
            dma((2, 2, LOCAL_HEADS)),
            dma((3,)),
            dma((3,)),
            dma((NY - 1,)),
            dma((NY - 1,)),
            dma((PHASES,)),
            dma((PHASES,)),
            dma((PHASES,)),
            dma((PHASES,)),
            dma((NZ,)),
            dma((NZ,)),
            dma((PHASES, 7)),
            dma((PHASES, 7)),
        ],
        compiler_params=pltpu.CompilerParams(
            collective_id=0, has_side_effects=True, vmem_limit_bytes=60 * 1024 * 1024
        ),
        name="vision_block",
    )(
        counts,
        patches.T,
        jnp.transpose(in_weight, (1, 2, 0)).reshape(3 * BLOCK, D),
        out_weight.T,
        vec,
        mw,
        merger_bias.reshape(1, LLMW),
    )


def solution(mesh):
    return jax.shard_map(
        per_device,
        mesh=mesh,
        in_specs=(
            P("dp", "tensor"),
            P(),
            P(),
            P(),
            P(None, None, "tensor"),
            P(None, "tensor"),
            P(None, "tensor"),
            P("tensor"),
            P("tensor"),
            P("tensor"),
            P(None, "tensor", "dp"),
            P(),
        ),
        out_specs=P(("dp", "tensor"), None),
        check_vma=False,
    )
```

```python
import functools
import math

import jax
import jax.numpy as jnp
from jax import lax
from jax.experimental import pallas as pl
from jax.experimental.pallas import tpu as pltpu
from jax.sharding import PartitionSpec as P

D = 1280
HEADS = 16
TILE = 512
NX = 4
NY = 4
NZ = 16
BLOCK = D // NX
HEAD = D // HEADS
LOCAL_HEADS = BLOCK // HEAD
LLMW = 4096
MROWS = TILE // 4
HALF = MROWS // 2
QUARTER = HALF // 2
ZCOLS = LLMW // NZ
PHASES = NZ // 2

EPS = 1e-06
MASKED = -1e30
MESH = pl.DeviceIdType.MESH
F32 = jnp.float32
BF16 = jnp.bfloat16
CHUNK = 80
SPLIT = 384

NT = (((1,), (1,)), ((), ()))
TN = (((0,), (0,)), ((), ()))


def kernel(
    counts_hbm,
    patches,
    in_w_hbm,
    out_w_hbm,
    gain1,
    shift1,
    in_bias,
    out_bias,
    gain2,
    shift2,
    mw_hbm,
    mbias_hbm,
    out,
    slot0,
    slot1,
    xbuf,
    hbuf,
    in_w,
    out_w,
    vec,
    vec2,
    in_b,
    vt,
    vt2,
    vt3,
    mw,
    mbias,
    normed,
    proj,
    stat,
    resid,
    wbuf,
    merged,
    pbuf,
    xpb,
    rel_a,
    rel_b,
    rs_a,
    rs_b,
    fa1,
    fa2,
    fb1,
    fb2,
    obuf,
    counts,
    local_sem,
    out_sem,
    part_send,
    part_recv,
    g_send,
    g_recv,
    h_send,
    h_recv,
    st_send,
    st_recv,
    ya_send,
    ya_recv,
    yb_send,
    yb_recv,
    za_send,
    za_recv,
    zb_send,
    zb_recv,
    pf_send,
    pf_recv,
    rs_send,
    rs_recv,
):
    rank = lax.axis_index("dp")
    t = lax.axis_index("tensor")
    c = lax.rem(rank, 2)
    y = lax.rem(rank // 2, NY)
    z = rank // (2 * NY)
    partner = rank + 1 - 2 * c
    right = lax.rem(t + 1, NX)
    left = lax.rem(t + NX - 1, NX)
    across = lax.rem(t + 2, NX)

    def zwrap(k):
        return lax.rem(k + NZ, NZ)

    def rank_of(zz, yy):
        return (zz * NY + yy) * 2 + c

    up = rank_of(zwrap(z + 1), y)
    down = rank_of(zwrap(z - 1), y)

    peers = [(rank, right), (rank, left), (partner, right), (partner, left), (rank, across), (partner, t)]
    peers += [(rank_of(z, lax.rem(y + dy, NY)), t) for dy in range(1, NY)]
    peers += [(up, t), (down, t)]
    barrier = pltpu.get_barrier_semaphore()
    for peer in peers:
        pl.semaphore_signal(barrier, inc=1, device_id=peer, device_id_type=MESH)

    def load(src, dst, index):
        copy = pltpu.make_async_copy(src, dst, local_sem.at[index])
        copy.start()
        return copy

    mw_copy = load(mw_hbm, mw, 0)
    first = load(patches.at[:, pl.ds(0, TILE)], slot0, 1)
    counted = load(counts_hbm, counts, 15)
    small = [load(gain1, vec.at[0], 2), load(shift1, vec.at[1], 3)]
    small += [load(in_bias, in_b, 4)]
    small += [load(out_bias, vec2.at[3], 7), load(gain2, vec2.at[4], 8)]
    small += [load(shift2, vec2.at[5], 9), load(mbias_hbm, mbias.at[0], 10)]
    win_copies = [load(in_w_hbm.at[k], in_w.at[:, k], 11 + k) for k in range(3)]
    wout_copy = load(out_w_hbm, out_w, 14)
    mw_copy.wait()
    wbuf[z, y, c] = jnp.concatenate([mw[j] for j in range(4)], axis=1)
    for copy in small:
        copy.wait()
    vt[...] = jnp.transpose(vec[...])
    vt2[...] = jnp.transpose(vec2[...])
    vt3[...] = jnp.transpose(jnp.concatenate([in_b[...], jnp.zeros((5, BLOCK), F32)], axis=0))

    pl.semaphore_wait(barrier, len(peers))

    def remote(src, dst, send, recv, device):
        return pltpu.make_async_remote_copy(
            src_ref=src, dst_ref=dst, send_sem=send, recv_sem=recv, device_id=device, device_id_type=MESH
        )

    def send(*args):
        copy = remote(*args)
        copy.start()

    swap = remote(patches.at[:, pl.ds(TILE, TILE)], slot1, part_send, part_recv, (partner, t))
    swap.start()

    def sub(buf, owner, h):
        return buf.at[pl.ds(pl.multiple_of(owner * BLOCK + h * HEAD, 16), HEAD)]

    def gather_copy(buf, send, recv, owner, h, way, hop):
        ref = sub(buf, owner, h)
        return remote(ref, ref, send, recv.at[way, hop, h], (rank, right if way == 0 else left))

    def gather_wait(buf, send, recv, h, way, hop):
        owner = lax.rem(t + (NX - 1 - hop if way == 0 else 1 + hop), NX)
        ref = sub(buf, owner, h)
        remote(ref, ref, send, recv.at[way, hop, h], (rank, right)).wait_recv()

    def own_send(buf, send, recv, h, way):
        copy = gather_copy(buf, send, recv, t, h, way, 0)
        copy.start()

    def forward(buf, send, recv, h):
        way = h % 2
        gather_wait(buf, send, recv, h, way, 0)
        owner = left if way == 0 else right
        copy = gather_copy(buf, send, recv, owner, h, way, 1)
        copy.start()

    def near_wait(buf, send, recv):
        for h in range(LOCAL_HEADS):
            gather_wait(buf, send, recv, h, 1 - h % 2, 0)

    def far_wait(buf, send, recv):
        for h in range(LOCAL_HEADS):
            gather_wait(buf, send, recv, h, h % 2, 1)

    half_a, half_b = pl.ds(0, SPLIT), pl.ds(SPLIT, D - SPLIT)

    def arrived(ref, recv):
        remote(ref, ref, part_send, recv, (partner, t)).wait_recv()

    def z_step(k):
        for way, device in ((0, up), (1, down)):
            if k > PHASES - way:
                continue
            zz = zwrap(z - (k - 1)) if way == 0 else zwrap(z + (k - 1))
            ref = wbuf.at[zz, :, c, :, half_a]
            send(ref, ref, za_send, za_recv.at[way, k - 1], (device, t))

    def z_step_b(k):
        for way, device in ((0, up), (1, down)):
            if k > PHASES - way:
                continue
            zz = zwrap(z - (k - 1)) if way == 0 else zwrap(z + (k - 1))
            ref = wbuf.at[zz, y, c, :, half_b]
            send(ref, ref, zb_send, zb_recv.at[way, k - 1], (device, t))

    def blocks_of(k):
        if k == 0:
            return ((0, z),)
        if k == PHASES:
            return ((2 * PHASES - 1, zwrap(z - PHASES)),)
        return ((2 * k - 1, zwrap(z - k)), (2 * k, zwrap(z + k)))

    def y_block(zz, dy):
        return wbuf.at[zz, lax.rem(y + NY - dy, NY), c, :, half_b]

    def y_peer(dy):
        return (rank_of(z, lax.rem(y + dy, NY)), t)

    def y_send_b(k):
        for index, zz in blocks_of(k):
            ref = y_block(zz, 0)
            for dy in (1, 3):
                send(ref, ref, yb_send, yb_recv.at[index, dy - 1], y_peer(dy))

    def y_forward(k):
        for turn, (index, zz) in enumerate(blocks_of(k)):
            arrived(y_block(zz, 1), yb_recv.at[index, 0])
            arrived(y_block(zz, 3), yb_recv.at[index, 2])
            dy = 1 if turn == 0 else 3
            ref = y_block(zz, dy)
            send(ref, ref, yb_send, yb_recv.at[index, 1], y_peer(dy))

    def hand_over(k):
        for index, zz in blocks_of(k):
            arrived(y_block(zz, 2), yb_recv.at[index, 1])
            ref = wbuf.at[zz, :, c]
            send(ref, ref, pf_send, pf_recv.at[index], (partner, t))

    def hand_wait(k):
        for index, zz in blocks_of(k):
            arrived(wbuf.at[zz, :, 1 - c], pf_recv.at[index])

    def weights_begin():
        ref = wbuf.at[z, y, c, :, half_a]
        for dy in (1, 3, 2):
            send(ref, ref, ya_send, ya_recv.at[dy - 1], (rank_of(z, lax.rem(y + dy, NY)), t))
        z_step_b(1)
        y_send_b(0)

    def weights_first():
        for dy in range(1, NY):
            arrived(wbuf.at[z, lax.rem(y + NY - dy, NY), c, :, half_a], ya_recv.at[dy - 1])
        z_step(1)

    def weights_step(k):
        if k <= PHASES:
            for way, (index, zz) in enumerate(blocks_of(k)):
                arrived(wbuf.at[zz, y, c, :, half_b], zb_recv.at[way, k - 1])
                arrived(wbuf.at[zz, :, c, :, half_a], za_recv.at[way, k - 1])
            z_step(k + 1)
            z_step_b(k + 1)
            y_send_b(k)
        if k - 1 <= PHASES:
            y_forward(k - 1)
        if k >= 2:
            hand_over(k - 2)

    counted.wait()
    own0 = counts[2 * rank]
    other1 = counts[2 * partner + 1]
    tile_count = jnp.where(own0 > 0, own0, other1)
    weights_begin()
    first.wait()
    swap.wait_recv()

    def choose(i, carry):
        rows = pl.ds(pl.multiple_of(i * CHUNK, 16), CHUNK)
        pick = jnp.full((CHUNK, TILE), own0, jnp.int32) > 0
        value = jnp.where(pick, slot0[rows, :].astype(F32), slot1[rows, :].astype(F32))
        xbuf[pl.ds(pl.multiple_of(t * BLOCK + i * CHUNK, 16), CHUNK), :] = value.astype(BF16)
        return carry

    lax.fori_loop(0, BLOCK // CHUNK, choose, 0)
    for h in (0, 2, 1, 3):
        own_send(xbuf, g_send, g_recv, h, 0)
        own_send(xbuf, g_send, g_recv, (h + 1) if h % 2 == 0 else (h - 1), 1)
    weights_first()

    def block_stats(owner):
        base = owner * BLOCK

        def total_of(i, acc):
            x = xbuf[pl.ds(pl.multiple_of(base + i * CHUNK, 16), CHUNK), :].astype(F32)
            return acc + jnp.sum(x, axis=0, keepdims=True)

        centre = lax.fori_loop(0, BLOCK // CHUNK, total_of, zero_row) * (1.0 / BLOCK)

        def spread_of(i, acc):
            x = xbuf[pl.ds(pl.multiple_of(base + i * CHUNK, 16), CHUNK), :].astype(F32) - centre
            return acc + jnp.sum(x * x, axis=0, keepdims=True)

        return centre, lax.fori_loop(0, BLOCK // CHUNK, spread_of, zero_row)

    zero_row = jnp.zeros((1, TILE), F32)
    stats = [block_stats(t)]
    for h in range(LOCAL_HEADS):
        forward(xbuf, g_send, g_recv, h)
    weights_step(1)
    near_wait(xbuf, g_send, g_recv)
    stats += [block_stats(left), block_stats(right)]
    weights_step(2)
    far_wait(xbuf, g_send, g_recv)
    stats += [block_stats(across)]
    mean = (stats[0][0] + stats[1][0] + stats[2][0] + stats[3][0]) * (1.0 / NX)
    spread = zero_row
    for centre, squares in stats:
        off = centre - mean
        spread = spread + squares + float(BLOCK) * (off * off)
    inv = lax.rsqrt(spread * (1.0 / D) + EPS)

    def normalise(i, carry):
        rows = pl.ds(pl.multiple_of(i * CHUNK, 16), CHUNK)
        x = xbuf[rows, :].astype(F32)
        gain = vt[rows, 0:1]
        shift = vt[rows, 1:2]
        normed[rows, :] = ((x - mean) * inv * gain + shift).astype(BF16)
        return carry

    lax.fori_loop(0, D // CHUNK, normalise, 0)
    weights_step(3)

    for copy in win_copies:
        copy.wait()
    scale = 1.0 / math.sqrt(HEAD)

    def attend(h):
        got = jnp.dot(in_w[h].reshape(3 * HEAD, D), normed[...], preferred_element_type=F32)
        bias = jnp.concatenate([vt3[h * HEAD : (h + 1) * HEAD, k : k + 1] for k in range(3)], axis=0)
        proj[0 : 3 * HEAD, :] = (got + bias).astype(BF16)
        live = lax.broadcasted_iota(jnp.int32, (TILE, TILE // 2), 0) < tile_count

        def columns(i, carry):
            cols = pl.ds(pl.multiple_of(i * (TILE // 2), 128), TILE // 2)
            scores = lax.dot_general(
                proj[HEAD : 2 * HEAD, :], proj[0:HEAD, cols], TN, preferred_element_type=F32
            )
            scores = jnp.where(live, scores * scale, MASKED)
            highest = jnp.max(scores, axis=0, keepdims=True)
            raised = jnp.exp(scores - highest)
            weights = (raised * (1.0 / jnp.sum(raised, axis=0, keepdims=True))).astype(BF16)
            got = jnp.dot(proj[2 * HEAD : 3 * HEAD, :], weights, preferred_element_type=F32)
            hbuf[pl.ds(pl.multiple_of(t * BLOCK + h * HEAD, 16), HEAD), cols] = got.astype(BF16)
            return carry

        lax.fori_loop(0, 2, columns, 0)

    for h in range(LOCAL_HEADS):
        attend(h)
        own_send(hbuf, h_send, h_recv, h, 0)
        own_send(hbuf, h_send, h_recv, h, 1)
        if h == 2:
            weights_step(4)
        if h >= 2:
            forward(hbuf, h_send, h_recv, h - 2)
    forward(hbuf, h_send, h_recv, 2)
    weights_step(5)
    forward(hbuf, h_send, h_recv, 3)
    near_wait(hbuf, h_send, h_recv)
    weights_step(6)
    far_wait(hbuf, h_send, h_recv)

    wout_copy.wait()
    got = jnp.dot(out_w[...], hbuf[...], preferred_element_type=F32)
    resid[...] = xbuf[pl.ds(pl.multiple_of(t * BLOCK, 16), BLOCK), :].astype(F32) + got + vt2[:, 3:4]

    def sums_of(i, acc):
        x = resid[pl.ds(pl.multiple_of(i * CHUNK, 16), CHUNK), :]
        return acc[0] + jnp.sum(x, axis=0, keepdims=True), acc[1] + jnp.sum(x * x, axis=0, keepdims=True)

    row_sum, row_squares = lax.fori_loop(0, BLOCK // CHUNK, sums_of, (zero_row, zero_row))
    stat[3] = jnp.concatenate([row_sum, row_squares, jnp.zeros((6, TILE), F32)], axis=0)
    targets = (right, left, across)
    for k in range(3):
        send(stat.at[3], stat.at[k], st_send, st_recv.at[k], (rank, targets[k]))
    weights_step(7)
    for k in range(3):
        arrived(stat.at[k], st_recv.at[k])
    sums = stat[0] + stat[1] + stat[2] + stat[3]
    row_mean = sums[0:1] * (1.0 / D)
    second = sums[1:2] * (1.0 / D)
    inv2 = lax.rsqrt(second - row_mean * row_mean + EPS)

    def encode(i, carry):
        rows = pl.ds(pl.multiple_of(i * CHUNK, 16), CHUNK)
        x = resid[rows, :]
        value = (x - row_mean) * inv2 * vt2[rows, 4:5] + vt2[rows, 5:6]
        proj[rows, :] = value.astype(BF16)
        return carry

    lax.fori_loop(0, BLOCK // CHUNK, encode, 0)
    pieces = []
    for j in range(4):
        chosen = (
            lax.broadcasted_iota(jnp.int32, (MROWS, TILE), 1)
            == 4 * lax.broadcasted_iota(jnp.int32, (MROWS, TILE), 0) + j
        )
        pick = jnp.where(chosen, 1.0, 0.0).astype(BF16)
        pieces.append(lax.dot_general(pick, proj[0:BLOCK, :], NT, preferred_element_type=F32))
    merged[...] = jnp.concatenate(pieces, axis=1).astype(BF16)

    same = pl.multiple_of(lax.rem(t, 2) * HALF, 16)
    other = pl.multiple_of(HALF - lax.rem(t, 2) * HALF, 16)
    upper = t // 2
    right_up, left_up = right // 2, left // 2
    right_rank = rank + (partner - rank) * right_up
    left_rank = rank + (partner - rank) * left_up

    def rs_copies(s):
        a_same, b_same = pl.ds(same, QUARTER), pl.ds(pl.multiple_of(same + QUARTER, 16), QUARTER)
        a_other, b_other = pl.ds(other, QUARTER), pl.ds(pl.multiple_of(other + QUARTER, 16), QUARTER)
        return (
            remote(pbuf.at[s, a_same], rel_a.at[s], rs_send.at[0], rs_recv.at[s, 0], (rank, right)),
            remote(pbuf.at[s, b_same], rel_b.at[s], rs_send.at[1], rs_recv.at[s, 1], (rank, left)),
            remote(pbuf.at[s, b_other], fb1.at[s], rs_send.at[2], rs_recv.at[s, 2], (right_rank, right)),
            remote(pbuf.at[s, a_other], fa1.at[s], rs_send.at[3], rs_recv.at[s, 3], (left_rank, left)),
            remote(rs_a.at[s], fa2.at[s], rs_send.at[4], rs_recv.at[s, 4], (right_rank, right)),
            remote(rs_b.at[s], fb2.at[s], rs_send.at[5], rs_recv.at[s, 5], (left_rank, left)),
            remote(pbuf.at[s, pl.ds(same, HALF)], xpb.at[s], rs_send.at[6], rs_recv.at[s, 6], (partner, t)),
        )

    def z_of(s):
        return (zwrap(z - s), zwrap(z + s)) if s else (z, zwrap(z - PHASES))

    def project(s):
        for k, zz in enumerate(z_of(s)):
            part = wbuf[zz].reshape(ZCOLS, D)
            got = lax.dot_general(merged[...], part, NT, preferred_element_type=F32)
            pbuf[s, :, k * ZCOLS : (k + 1) * ZCOLS] = got.astype(BF16)
        copies = rs_copies(s)
        for k in (0, 1, 6):
            copies[k].start()

    def direct(s):
        copies = rs_copies(s)
        for k in (2, 3):
            copies[k].start()

    def relay(s):
        copies = rs_copies(s)
        copies[0].wait_recv()
        own = pbuf[s, pl.ds(other, QUARTER), :].astype(F32)
        rs_a[s] = (rel_a[s].astype(F32) + own).astype(BF16)
        copies[4].start()
        copies[1].wait_recv()
        own = pbuf[s, pl.ds(pl.multiple_of(other + QUARTER, 16), QUARTER), :].astype(F32)
        rs_b[s] = (rel_b[s].astype(F32) + own).astype(BF16)
        copies[5].start()

    my_count = counts[2 * rank + upper]
    written = []

    def collect(s):
        copies = rs_copies(s)
        for k in (2, 3, 4, 5, 6):
            copies[k].wait_recv()
        local = pbuf[s, pl.ds(same, HALF), :].astype(F32)
        passed = xpb[s].astype(F32)
        is_upper = jnp.full((HALF, 2 * ZCOLS), upper, jnp.int32) > 0
        total = jnp.where(is_upper, passed, local)
        top = fa1[s].astype(F32) + fa2[s].astype(F32)
        bottom = fb1[s].astype(F32) + fb2[s].astype(F32)
        total = total + jnp.concatenate([top, bottom], axis=0)
        row = lax.broadcasted_iota(jnp.int32, (HALF, ZCOLS), 0) + lax.rem(t, 2) * HALF
        keep = 4 * row < my_count
        for k, zz in enumerate(z_of(s)):
            cols = pl.ds(pl.multiple_of(zz * ZCOLS, 128), ZCOLS)
            value = total[:, k * ZCOLS : (k + 1) * ZCOLS] + mbias[:, cols]
            obuf[:, cols] = jnp.where(keep, value, 0.0).astype(BF16)
            copy = pltpu.make_async_copy(obuf.at[:, cols], out.at[:, cols], out_sem.at[s, k])
            copy.start()
            written.append(copy)

    order = (1, 2, 3, 4, 5, 6, 7, 0)
    for n, s in enumerate(order):
        hand_wait(s)
        if s == 0:
            hand_wait(PHASES)
        project(s)
        if n in (1, 3, 5):
            weights_step(8 + n // 2)
        if n >= 2:
            relay(order[n - 2])
        if n >= 4:
            direct(order[n - 4])
    relay(order[6])
    direct(order[4])
    relay(order[7])
    for n in (5, 6, 7):
        direct(order[n])
    for s in order:
        collect(s)

    def all_left(ref, sem):
        remote(ref, ref, sem, part_recv, (partner, t)).wait_send()

    swap.wait_send()
    all_left(xbuf.at[pl.ds(0, 3 * BLOCK)], g_send)
    all_left(hbuf.at[pl.ds(0, 3 * BLOCK)], h_send)
    all_left(stat.at[pl.ds(0, 3)], st_send)
    all_left(wbuf.at[pl.ds(0, NY - 1), y, c, :, half_a], ya_send)
    all_left(wbuf.at[pl.ds(0, 3 * NZ // 4), :, c, :, half_b], yb_send)
    all_left(wbuf.at[pl.ds(0, NZ - 1), :, c, :, half_a], za_send)
    all_left(wbuf.at[pl.ds(0, NZ - 1), y, c, :, half_b], zb_send)
    all_left(wbuf.at[:, :, c], pf_send)
    for k in range(6):
        all_left(rel_a, rs_send.at[k])
    all_left(xpb, rs_send.at[6])
    for copy in written:
        copy.wait()


def per_device(
    patches,
    counts,
    first_gain,
    first_shift,
    in_weight,
    in_bias,
    out_weight,
    out_bias,
    second_gain,
    second_shift,
    merger_weight,
    merger_bias,
):
    any_spec = pl.BlockSpec(memory_space=pl.ANY)
    dma = pltpu.SemaphoreType.DMA
    return pl.pallas_call(
        kernel,
        out_shape=jax.ShapeDtypeStruct((HALF, LLMW), BF16),
        in_specs=[any_spec] * 12,
        out_specs=any_spec,
        scratch_shapes=[
            pltpu.VMEM((BLOCK, TILE), BF16),
            pltpu.VMEM((BLOCK, TILE), BF16),
            pltpu.VMEM((D, TILE), BF16),
            pltpu.VMEM((D, TILE), BF16),
            pltpu.VMEM((LOCAL_HEADS, 3, HEAD, D), BF16),
            pltpu.VMEM((BLOCK, D), BF16),
            pltpu.VMEM((8, D), F32),
            pltpu.VMEM((8, BLOCK), F32),
            pltpu.VMEM((3, BLOCK), F32),
            pltpu.VMEM((D, 8), F32),
            pltpu.VMEM((BLOCK, 8), F32),
            pltpu.VMEM((BLOCK, 8), F32),
            pltpu.VMEM((4, LLMW // 128, BLOCK), BF16),
            pltpu.VMEM((1, LLMW), F32),
            pltpu.VMEM((D, TILE), BF16),
            pltpu.VMEM((3 * BLOCK, TILE), BF16),
            pltpu.VMEM((4, 8, TILE), F32),
            pltpu.VMEM((BLOCK, TILE), F32),
            pltpu.VMEM((NZ, NY, 2, 32, D), BF16),
            pltpu.VMEM((MROWS, D), BF16),
            pltpu.VMEM((PHASES, MROWS, 2 * ZCOLS), BF16),
            pltpu.VMEM((PHASES, HALF, 2 * ZCOLS), BF16),
        ]
        + [pltpu.VMEM((PHASES, QUARTER, 2 * ZCOLS), BF16)] * 8
        + [pltpu.VMEM((HALF, LLMW), BF16)]
        + [pltpu.SMEM((256,), jnp.int32)]
        + [dma((16,)), dma((PHASES, 2)), dma, dma]
        + [dma, dma((2, 2, LOCAL_HEADS))] * 2
        + [dma, dma((3,))] * 2
        + [dma, dma((NZ, 3))]
        + [dma, dma((2, PHASES))] * 2
        + [dma, dma((NZ,)), dma((7,)), dma((PHASES, 7))],
        compiler_params=pltpu.CompilerParams(
            collective_id=0, has_side_effects=True, vmem_limit_bytes=60 * 1024 * 1024
        ),
        name="vision_block",
    )(
        counts,
        patches.T,
        jnp.transpose(in_weight, (1, 2, 0)).reshape(3, LOCAL_HEADS, HEAD, D),
        out_weight.T,
        first_gain,
        first_shift,
        in_bias,
        out_bias,
        second_gain,
        second_shift,
        jnp.transpose(merger_weight, (0, 2, 1)),
        merger_bias,
    )


def solution(mesh):
    return jax.shard_map(
        per_device,
        mesh=mesh,
        in_specs=(
            P("dp", "tensor"),
            P(),
            P(),
            P(),
            P(None, None, "tensor"),
            P(None, "tensor"),
            P(None, "tensor"),
            P("tensor"),
            P("tensor"),
            P("tensor"),
            P(None, "tensor", "dp"),
            P(),
        ),
        out_specs=P(("dp", "tensor"), None),
        check_vma=False,
    )
```

```python
import functools
import math

import jax
import jax.numpy as jnp
from jax import lax
from jax.experimental import pallas as pl
from jax.experimental.pallas import tpu as pltpu
from jax.sharding import PartitionSpec as P

D = 1280
HEADS = 16
TILE = 512
NX = 4
NY = 4
NZ = 16
BLOCK = D // NX
HEAD = D // HEADS
LOCAL_HEADS = BLOCK // HEAD
LLMW = 4096
MROWS = TILE // 4
HALF = MROWS // 2
QUARTER = HALF // 2
ZCOLS = LLMW // NZ
PHASES = NZ // 2

EPS = 1e-06
MASKED = -1e30
MESH = pl.DeviceIdType.MESH
F32 = jnp.float32
BF16 = jnp.bfloat16
CHUNK = 80
SPLIT = 512

NT = (((1,), (1,)), ((), ()))
TN = (((0,), (0,)), ((), ()))


def kernel(
    counts_hbm,
    patches,
    in_w_hbm,
    out_w_hbm,
    gain1,
    shift1,
    in_bias,
    out_bias,
    gain2,
    shift2,
    mw_hbm,
    mbias_hbm,
    out,
    slot0,
    slot1,
    xbuf,
    hbuf,
    in_w,
    out_w,
    vec,
    vec2,
    in_b,
    vt,
    vt2,
    vt3,
    mw,
    mbias,
    normed,
    proj,
    stat,
    resid,
    wbuf,
    merged,
    pbuf,
    xpb,
    rel_a,
    rel_b,
    rs_a,
    rs_b,
    fa1,
    fa2,
    fb1,
    fb2,
    last,
    obuf,
    counts,
    local_sem,
    out_sem,
    part_send,
    part_recv,
    g_send,
    g_recv,
    h_send,
    h_recv,
    st_send,
    st_recv,
    ya_send,
    ya_recv,
    yb_send,
    yb_recv,
    za_send,
    za_recv,
    zb_send,
    zb_recv,
    pf_send,
    pf_recv,
    rs_send,
    rs_recv,
    last_send,
    last_recv,
):
    rank = lax.axis_index("dp")
    t = lax.axis_index("tensor")
    c = lax.rem(rank, 2)
    y = lax.rem(rank // 2, NY)
    z = rank // (2 * NY)
    partner = rank + 1 - 2 * c
    right = lax.rem(t + 1, NX)
    left = lax.rem(t + NX - 1, NX)
    across = lax.rem(t + 2, NX)

    def zwrap(k):
        return lax.rem(k + NZ, NZ)

    def rank_of(zz, yy):
        return (zz * NY + yy) * 2 + c

    up = rank_of(zwrap(z + 1), y)
    down = rank_of(zwrap(z - 1), y)

    peers = [(rank, right), (rank, left), (partner, right), (partner, left), (rank, across), (partner, across), (partner, t)]
    peers += [(rank_of(z, lax.rem(y + dy, NY)), t) for dy in range(1, NY)]
    peers += [(up, t), (down, t)]
    barrier = pltpu.get_barrier_semaphore()
    for peer in peers:
        pl.semaphore_signal(barrier, inc=1, device_id=peer, device_id_type=MESH)

    def load(src, dst, index):
        copy = pltpu.make_async_copy(src, dst, local_sem.at[index])
        copy.start()
        return copy

    mw_copy = load(mw_hbm, mw, 0)
    first = load(patches.at[:, pl.ds(0, TILE)], slot0, 1)
    counted = load(counts_hbm, counts, 15)
    small = [load(gain1, vec.at[0], 2), load(shift1, vec.at[1], 3)]
    small += [load(in_bias, in_b, 4)]
    small += [load(out_bias, vec2.at[3], 7), load(gain2, vec2.at[4], 8)]
    small += [load(shift2, vec2.at[5], 9), load(mbias_hbm, mbias.at[0], 10)]
    win_copies = [load(in_w_hbm.at[k], in_w.at[:, k], 11 + k) for k in range(3)]
    wout_copy = load(out_w_hbm, out_w, 14)
    pl.semaphore_wait(barrier, len(peers))

    def remote(src, dst, send, recv, device):
        return pltpu.make_async_remote_copy(
            src_ref=src, dst_ref=dst, send_sem=send, recv_sem=recv, device_id=device, device_id_type=MESH
        )

    def send(*args):
        copy = remote(*args)
        copy.start()

    def piece(i):
        return pl.ds(i * HEAD, HEAD)

    swaps = [
        remote(patches.at[piece(i), pl.ds(TILE, TILE)], slot1.at[piece(i)], part_send.at[i], part_recv.at[i], (partner, t))
        for i in range(LOCAL_HEADS)
    ]
    for i in (0, 1, 2, 3):
        swaps[i].start()
    mw_copy.wait()
    wbuf[z, y, c] = jnp.concatenate([mw[j] for j in range(4)], axis=1)
    for copy in small:
        copy.wait()
    vt[...] = jnp.transpose(vec[...])
    vt2[...] = jnp.transpose(vec2[...])
    vt3[...] = jnp.transpose(jnp.concatenate([in_b[...], jnp.zeros((5, BLOCK), F32)], axis=0))

    def sub(buf, owner, h):
        return buf.at[pl.ds(pl.multiple_of(owner * BLOCK + h * HEAD, 16), HEAD)]

    def gather_copy(buf, send, recv, owner, h, way, hop):
        ref = sub(buf, owner, h)
        return remote(ref, ref, send, recv.at[way, hop, h], (rank, right if way == 0 else left))

    def gather_wait(buf, send, recv, h, way, hop):
        owner = lax.rem(t + (NX - 1 - hop if way == 0 else 1 + hop), NX)
        ref = sub(buf, owner, h)
        remote(ref, ref, send, recv.at[way, hop, h], (rank, right)).wait_recv()

    def own_send(buf, send, recv, h, way):
        copy = gather_copy(buf, send, recv, t, h, way, 0)
        copy.start()

    def forward(buf, send, recv, h):
        way = h % 2
        gather_wait(buf, send, recv, h, way, 0)
        owner = left if way == 0 else right
        copy = gather_copy(buf, send, recv, owner, h, way, 1)
        copy.start()

    def near_wait(buf, send, recv):
        for h in range(LOCAL_HEADS):
            gather_wait(buf, send, recv, h, 1 - h % 2, 0)

    def far_wait(buf, send, recv):
        for h in range(LOCAL_HEADS):
            gather_wait(buf, send, recv, h, h % 2, 1)

    half_a, half_b = pl.ds(0, SPLIT), pl.ds(SPLIT, D - SPLIT)

    def arrived(ref, recv):
        remote(ref, ref, g_send, recv, (partner, t)).wait_recv()

    def z_origin(way, k):
        return zwrap(z - k) if way == 0 else zwrap(z + k)

    def z_send_a(way, k):
        if k <= PHASES - way:
            ref = wbuf.at[z_origin(way, k - 1), :, c, :, half_a]
            send(ref, ref, za_send, za_recv.at[way, k - 1], ((up, down)[way], t))

    def z_send_b(way, k):
        if k <= PHASES - way:
            ref = wbuf.at[z_origin(way, k - 1), y, c, :, half_b]
            send(ref, ref, zb_send, zb_recv.at[way, k - 1], ((up, down)[way], t))

    def blocks_of(k):
        if k == 0:
            return ((0, z),)
        if k == PHASES:
            return ((2 * PHASES - 1, zwrap(z - PHASES)),)
        return ((2 * k - 1, zwrap(z - k)), (2 * k, zwrap(z + k)))

    def y_block(zz, dy):
        return wbuf.at[zz, lax.rem(y + NY - dy, NY), c, :, half_b]

    def y_peer(dy):
        return (rank_of(z, lax.rem(y + dy, NY)), t)

    def y_send_b(k):
        for index, zz in blocks_of(k):
            ref = y_block(zz, 0)
            for dy in (1, 3, 2):
                send(ref, ref, yb_send, yb_recv.at[index, dy - 1], y_peer(dy))

    def hand_over(k):
        for index, zz in blocks_of(k):
            for dy in (1, 3, 2):
                arrived(y_block(zz, dy), yb_recv.at[index, dy - 1])
            ref = wbuf.at[zz, :, c]
            send(ref, ref, pf_send, pf_recv.at[index], (partner, t))

    def hand_wait(k):
        for index, zz in blocks_of(k):
            arrived(wbuf.at[zz, :, 1 - c], pf_recv.at[index])

    def weights_begin():
        ref = wbuf.at[z, y, c, :, half_a]
        for dy in (1, 3, 2):
            send(ref, ref, ya_send, ya_recv.at[dy - 1], (rank_of(z, lax.rem(y + dy, NY)), t))
        z_send_b(0, 1)
        z_send_b(1, 1)
        y_send_b(0)

    def weights_first():
        for dy in range(1, NY):
            arrived(wbuf.at[z, lax.rem(y + NY - dy, NY), c, :, half_a], ya_recv.at[dy - 1])
        z_send_a(0, 1)
        z_send_a(1, 1)

    def weights_step(k):
        if k == 0:
            weights_first()
            return
        if k <= PHASES:
            for way, (index, zz) in enumerate(blocks_of(k)):
                arrived(wbuf.at[zz, :, c, :, half_a], za_recv.at[way, k - 1])
                z_send_a(way, k + 1)
            for way, (index, zz) in enumerate(blocks_of(k)):
                arrived(wbuf.at[zz, y, c, :, half_b], zb_recv.at[way, k - 1])
                z_send_b(way, k + 1)
        if k <= PHASES:
            y_send_b(k)
        hand_over(k - 1)

    counted.wait()
    own0 = counts[2 * rank]
    other1 = counts[2 * partner + 1]
    tile_count = jnp.where(own0 > 0, own0, other1)
    first.wait()
    weights_begin()
    own_live = jnp.full((HEAD, TILE), own0, jnp.int32) > 0

    def choose(i):
        swaps[i].wait_recv()
        value = jnp.where(own_live, slot0[piece(i), :].astype(F32), slot1[piece(i), :].astype(F32))
        xbuf[pl.ds(pl.multiple_of(t * BLOCK + i * HEAD, 16), HEAD), :] = value.astype(BF16)

    for i in range(LOCAL_HEADS):
        choose(i)
    for h in (0, 2, 1, 3):
        own_send(xbuf, g_send, g_recv, h, 0)
        own_send(xbuf, g_send, g_recv, (h + 1) if h % 2 == 0 else (h - 1), 1)
    weights_step(0)

    def block_stats(owner):
        base = owner * BLOCK

        def total_of(i, acc):
            x = xbuf[pl.ds(pl.multiple_of(base + i * CHUNK, 16), CHUNK), :].astype(F32)
            return acc + jnp.sum(x, axis=0, keepdims=True)

        centre = lax.fori_loop(0, BLOCK // CHUNK, total_of, zero_row) * (1.0 / BLOCK)

        def spread_of(i, acc):
            x = xbuf[pl.ds(pl.multiple_of(base + i * CHUNK, 16), CHUNK), :].astype(F32) - centre
            return acc + jnp.sum(x * x, axis=0, keepdims=True)

        return centre, lax.fori_loop(0, BLOCK // CHUNK, spread_of, zero_row)

    zero_row = jnp.zeros((1, TILE), F32)
    stats = [block_stats(t)]
    for h in range(LOCAL_HEADS):
        forward(xbuf, g_send, g_recv, h)
    weights_step(1)
    near_wait(xbuf, g_send, g_recv)
    stats += [block_stats(left), block_stats(right)]
    weights_step(2)
    far_wait(xbuf, g_send, g_recv)
    stats += [block_stats(across)]
    mean = (stats[0][0] + stats[1][0] + stats[2][0] + stats[3][0]) * (1.0 / NX)
    spread = zero_row
    for centre, squares in stats:
        off = centre - mean
        spread = spread + squares + float(BLOCK) * (off * off)
    inv = lax.rsqrt(spread * (1.0 / D) + EPS)

    def normalise(i, carry):
        rows = pl.ds(pl.multiple_of(i * CHUNK, 16), CHUNK)
        x = xbuf[rows, :].astype(F32)
        gain = vt[rows, 0:1]
        shift = vt[rows, 1:2]
        normed[rows, :] = ((x - mean) * inv * gain + shift).astype(BF16)
        return carry

    lax.fori_loop(0, D // CHUNK, normalise, 0)

    for copy in win_copies:
        copy.wait()
    scale = 1.0 / math.sqrt(HEAD)

    def attend(h):
        got = jnp.dot(in_w[h].reshape(3 * HEAD, D), normed[...], preferred_element_type=F32)
        bias = jnp.concatenate([vt3[h * HEAD : (h + 1) * HEAD, k : k + 1] for k in range(3)], axis=0)
        proj[0 : 3 * HEAD, :] = (got + bias).astype(BF16)
        live = lax.broadcasted_iota(jnp.int32, (TILE, TILE // 2), 0) < tile_count

        def columns(i, carry):
            cols = pl.ds(pl.multiple_of(i * (TILE // 2), 128), TILE // 2)
            scores = lax.dot_general(
                proj[HEAD : 2 * HEAD, :], proj[0:HEAD, cols], TN, preferred_element_type=F32
            )
            scores = jnp.where(live, scores * scale, MASKED)
            highest = jnp.max(scores, axis=0, keepdims=True)
            raised = jnp.exp(scores - highest)
            weights = (raised * (1.0 / jnp.sum(raised, axis=0, keepdims=True))).astype(BF16)
            got = jnp.dot(proj[2 * HEAD : 3 * HEAD, :], weights, preferred_element_type=F32)
            hbuf[pl.ds(pl.multiple_of(t * BLOCK + h * HEAD, 16), HEAD), cols] = got.astype(BF16)
            return carry

        lax.fori_loop(0, 2, columns, 0)

    for h in range(LOCAL_HEADS):
        attend(h)
        own_send(hbuf, h_send, h_recv, h, 0)
        own_send(hbuf, h_send, h_recv, h, 1)
        if h == 1:
            weights_step(3)
        if h >= 2:
            forward(hbuf, h_send, h_recv, h - 2)
    weights_step(4)
    forward(hbuf, h_send, h_recv, 2)
    forward(hbuf, h_send, h_recv, 3)
    near_wait(hbuf, h_send, h_recv)
    weights_step(5)
    far_wait(hbuf, h_send, h_recv)

    wout_copy.wait()
    got = jnp.dot(out_w[...], hbuf[...], preferred_element_type=F32)
    resid[...] = xbuf[pl.ds(pl.multiple_of(t * BLOCK, 16), BLOCK), :].astype(F32) + got + vt2[:, 3:4]

    def sums_of(i, acc):
        x = resid[pl.ds(pl.multiple_of(i * CHUNK, 16), CHUNK), :]
        return acc[0] + jnp.sum(x, axis=0, keepdims=True), acc[1] + jnp.sum(x * x, axis=0, keepdims=True)

    row_sum, row_squares = lax.fori_loop(0, BLOCK // CHUNK, sums_of, (zero_row, zero_row))
    stat[3] = jnp.concatenate([row_sum, row_squares, jnp.zeros((6, TILE), F32)], axis=0)
    targets = (right, left, across)
    for k in range(3):
        send(stat.at[3], stat.at[k], st_send, st_recv.at[k], (rank, targets[k]))
    weights_step(6)
    for k in range(3):
        arrived(stat.at[k], st_recv.at[k])
    sums = stat[0] + stat[1] + stat[2] + stat[3]
    row_mean = sums[0:1] * (1.0 / D)
    second = sums[1:2] * (1.0 / D)
    inv2 = lax.rsqrt(second - row_mean * row_mean + EPS)

    def encode(i, carry):
        rows = pl.ds(pl.multiple_of(i * CHUNK, 16), CHUNK)
        x = resid[rows, :]
        value = (x - row_mean) * inv2 * vt2[rows, 4:5] + vt2[rows, 5:6]
        proj[rows, :] = value.astype(BF16)
        return carry

    lax.fori_loop(0, BLOCK // CHUNK, encode, 0)
    pieces = []
    for j in range(4):
        chosen = (
            lax.broadcasted_iota(jnp.int32, (MROWS, TILE), 1)
            == 4 * lax.broadcasted_iota(jnp.int32, (MROWS, TILE), 0) + j
        )
        pick = jnp.where(chosen, 1.0, 0.0).astype(BF16)
        pieces.append(lax.dot_general(pick, proj[0:BLOCK, :], NT, preferred_element_type=F32))
    merged[...] = jnp.concatenate(pieces, axis=1).astype(BF16)

    same = pl.multiple_of(lax.rem(t, 2) * HALF, 16)
    other = pl.multiple_of(HALF - lax.rem(t, 2) * HALF, 16)
    upper = t // 2
    right_up, left_up = right // 2, left // 2
    right_rank = rank + (partner - rank) * right_up
    left_rank = rank + (partner - rank) * left_up
    across_rank = rank + (partner - rank) * (across // 2)

    def rs_copies(s):
        a_same, b_same = pl.ds(same, QUARTER), pl.ds(pl.multiple_of(same + QUARTER, 16), QUARTER)
        a_other, b_other = pl.ds(other, QUARTER), pl.ds(pl.multiple_of(other + QUARTER, 16), QUARTER)
        return (
            remote(pbuf.at[s, a_same], rel_a.at[s], rs_send.at[0], rs_recv.at[s, 0], (rank, right)),
            remote(pbuf.at[s, b_same], rel_b.at[s], rs_send.at[1], rs_recv.at[s, 1], (rank, left)),
            remote(pbuf.at[s, b_other], fb1.at[s], rs_send.at[2], rs_recv.at[s, 2], (right_rank, right)),
            remote(pbuf.at[s, a_other], fa1.at[s], rs_send.at[3], rs_recv.at[s, 3], (left_rank, left)),
            remote(rs_a.at[s], fa2.at[s], rs_send.at[4], rs_recv.at[s, 4], (right_rank, right)),
            remote(rs_b.at[s], fb2.at[s], rs_send.at[5], rs_recv.at[s, 5], (left_rank, left)),
            remote(pbuf.at[s, pl.ds(same, HALF)], xpb.at[s], rs_send.at[6], rs_recv.at[s, 6], (partner, t)),
        )

    def z_of(s):
        return (zwrap(z - s), zwrap(z + s)) if s else (z, zwrap(z - PHASES))

    def project(s):
        for k, zz in enumerate(z_of(s)):
            part = wbuf[zz].reshape(ZCOLS, D)
            got = lax.dot_general(merged[...], part, NT, preferred_element_type=F32)
            pbuf[s, :, k * ZCOLS : (k + 1) * ZCOLS] = got.astype(BF16)
        copies = rs_copies(s)
        for k in (0, 1, 6) if s else (6,):
            copies[k].start()

    def last_copies():
        mine_rows, their_rows = pl.ds(same, HALF), pl.ds(other, HALF)
        return (
            remote(pbuf.at[0, mine_rows], last.at[0], last_send, last_recv.at[0], (across_rank, across)),
            remote(pbuf.at[0, their_rows], last.at[1], last_send, last_recv.at[1], (right_rank, right)),
            remote(pbuf.at[0, their_rows], last.at[2], last_send, last_recv.at[2], (left_rank, left)),
        )

    def direct(s):
        copies = rs_copies(s)
        for k in (2, 3):
            copies[k].start()

    def relay(s):
        copies = rs_copies(s)
        copies[0].wait_recv()
        own = pbuf[s, pl.ds(other, QUARTER), :].astype(F32)
        rs_a[s] = (rel_a[s].astype(F32) + own).astype(BF16)
        copies[4].start()
        copies[1].wait_recv()
        own = pbuf[s, pl.ds(pl.multiple_of(other + QUARTER, 16), QUARTER), :].astype(F32)
        rs_b[s] = (rel_b[s].astype(F32) + own).astype(BF16)
        copies[5].start()

    my_count = counts[2 * rank + upper]
    written = []

    def collect(s):
        copies = rs_copies(s)
        for k in (2, 3, 4, 5, 6) if s else (6,):
            copies[k].wait_recv()
        if s == 0:
            for copy in last_copies():
                copy.wait_recv()
        local = pbuf[s, pl.ds(same, HALF), :].astype(F32)
        passed = xpb[s].astype(F32)
        is_upper = jnp.full((HALF, 2 * ZCOLS), upper, jnp.int32) > 0
        total = jnp.where(is_upper, passed, local)
        if s == 0:
            total = total + last[0].astype(F32) + last[1].astype(F32) + last[2].astype(F32)
        else:
            top = fa1[s].astype(F32) + fa2[s].astype(F32)
            bottom = fb1[s].astype(F32) + fb2[s].astype(F32)
            total = total + jnp.concatenate([top, bottom], axis=0)
        row = lax.broadcasted_iota(jnp.int32, (HALF, ZCOLS), 0) + lax.rem(t, 2) * HALF
        keep = 4 * row < my_count
        for k, zz in enumerate(z_of(s)):
            cols = pl.ds(pl.multiple_of(zz * ZCOLS, 128), ZCOLS)
            value = total[:, k * ZCOLS : (k + 1) * ZCOLS] + mbias[:, cols]
            obuf[:, cols] = jnp.where(keep, value, 0.0).astype(BF16)
            copy = pltpu.make_async_copy(obuf.at[:, cols], out.at[:, cols], out_sem.at[s, k])
            copy.start()
            written.append(copy)

    def phase(s):
        hand_wait(s)
        if s == 0:
            hand_wait(PHASES)
        project(s)

    for s in (1, 2, 3, 4, 5):
        phase(s)
    weights_step(7)
    for s in (1, 2, 3):
        relay(s)
        direct(s)
    phase(6)
    relay(4)
    direct(4)
    weights_step(8)
    relay(5)
    phase(7)
    direct(5)
    direct(6)
    relay(6)
    weights_step(9)
    phase(0)
    for copy in last_copies():
        copy.start()
    relay(7)
    direct(7)
    for s in (1, 2, 3, 4, 5, 6, 0, 7):
        collect(s)

    def all_left(ref, sem):
        remote(ref, ref, sem, part_recv.at[0], (partner, t)).wait_send()

    for copy in swaps:
        copy.wait_send()
    all_left(xbuf.at[pl.ds(0, 3 * BLOCK)], g_send)
    all_left(hbuf.at[pl.ds(0, 3 * BLOCK)], h_send)
    all_left(stat.at[pl.ds(0, 3)], st_send)
    all_left(wbuf.at[pl.ds(0, NY - 1), y, c, :, half_a], ya_send)
    all_left(wbuf.at[pl.ds(0, 3 * NZ // 4), :, c, :, half_b], yb_send)
    all_left(wbuf.at[pl.ds(0, NZ - 1), :, c, :, half_a], za_send)
    all_left(wbuf.at[pl.ds(0, NZ - 1), y, c, :, half_b], zb_send)
    all_left(wbuf.at[:, :, c], pf_send)
    for k in range(6):
        all_left(rel_a.at[pl.ds(0, PHASES - 1)], rs_send.at[k])
    all_left(last, last_send)
    all_left(xpb, rs_send.at[6])
    for copy in written:
        copy.wait()


def per_device(
    patches,
    counts,
    first_gain,
    first_shift,
    in_weight,
    in_bias,
    out_weight,
    out_bias,
    second_gain,
    second_shift,
    merger_weight,
    merger_bias,
):
    any_spec = pl.BlockSpec(memory_space=pl.ANY)
    dma = pltpu.SemaphoreType.DMA
    return pl.pallas_call(
        kernel,
        out_shape=jax.ShapeDtypeStruct((HALF, LLMW), BF16),
        in_specs=[any_spec] * 12,
        out_specs=any_spec,
        scratch_shapes=[
            pltpu.VMEM((BLOCK, TILE), BF16),
            pltpu.VMEM((BLOCK, TILE), BF16),
            pltpu.VMEM((D, TILE), BF16),
            pltpu.VMEM((D, TILE), BF16),
            pltpu.VMEM((LOCAL_HEADS, 3, HEAD, D), BF16),
            pltpu.VMEM((BLOCK, D), BF16),
            pltpu.VMEM((8, D), F32),
            pltpu.VMEM((8, BLOCK), F32),
            pltpu.VMEM((3, BLOCK), F32),
            pltpu.VMEM((D, 8), F32),
            pltpu.VMEM((BLOCK, 8), F32),
            pltpu.VMEM((BLOCK, 8), F32),
            pltpu.VMEM((4, LLMW // 128, BLOCK), BF16),
            pltpu.VMEM((1, LLMW), F32),
            pltpu.VMEM((D, TILE), BF16),
            pltpu.VMEM((3 * BLOCK, TILE), BF16),
            pltpu.VMEM((4, 8, TILE), F32),
            pltpu.VMEM((BLOCK, TILE), F32),
            pltpu.VMEM((NZ, NY, 2, 32, D), BF16),
            pltpu.VMEM((MROWS, D), BF16),
            pltpu.VMEM((PHASES, MROWS, 2 * ZCOLS), BF16),
            pltpu.VMEM((PHASES, HALF, 2 * ZCOLS), BF16),
        ]
        + [pltpu.VMEM((PHASES, QUARTER, 2 * ZCOLS), BF16)] * 8
        + [pltpu.VMEM((3, HALF, 2 * ZCOLS), BF16)]
        + [pltpu.VMEM((HALF, LLMW), BF16)]
        + [pltpu.SMEM((256,), jnp.int32)]
        + [dma((16,)), dma((PHASES, 2)), dma((LOCAL_HEADS,)), dma((LOCAL_HEADS,))]
        + [dma, dma((2, 2, LOCAL_HEADS))] * 2
        + [dma, dma((3,))]
        + [dma, dma((3,))]
        + [dma, dma((NZ, 3))]
        + [dma, dma((2, PHASES))] * 2
        + [dma, dma((NZ,)), dma((7,)), dma((PHASES, 7)), dma, dma((3,))],
        compiler_params=pltpu.CompilerParams(
            collective_id=0, has_side_effects=True, vmem_limit_bytes=60 * 1024 * 1024
        ),
        name="vision_block",
    )(
        counts,
        patches.T,
        jnp.transpose(in_weight, (1, 2, 0)).reshape(3, LOCAL_HEADS, HEAD, D),
        out_weight.T,
        first_gain,
        first_shift,
        in_bias,
        out_bias,
        second_gain,
        second_shift,
        jnp.transpose(merger_weight, (0, 2, 1)),
        merger_bias,
    )


def solution(mesh):
    return jax.shard_map(
        per_device,
        mesh=mesh,
        in_specs=(
            P("dp", "tensor"),
            P(),
            P(),
            P(),
            P(None, None, "tensor"),
            P(None, "tensor"),
            P(None, "tensor"),
            P("tensor"),
            P("tensor"),
            P("tensor"),
            P(None, "tensor", "dp"),
            P(),
        ),
        out_specs=P(("dp", "tensor"), None),
        check_vma=False,
    )
```

```python
import functools
import math

import jax
import jax.numpy as jnp
from jax import lax
from jax.experimental import pallas as pl
from jax.experimental.pallas import tpu as pltpu
from jax.sharding import PartitionSpec as P

D = 1280
HEADS = 16
TILE = 512
NX = 4
NY = 4
NZ = 16
BLOCK = D // NX
HEAD = D // HEADS
LOCAL_HEADS = BLOCK // HEAD
LLMW = 4096
MROWS = TILE // 4
HALF = MROWS // 2
QUARTER = HALF // 2
ZCOLS = LLMW // NZ
PHASES = NZ // 2

EPS = 1e-06
MASKED = -1e30
MESH = pl.DeviceIdType.MESH
F32 = jnp.float32
BF16 = jnp.bfloat16
CHUNK = 80
SPLIT = 512

NT = (((1,), (1,)), ((), ()))
TN = (((0,), (0,)), ((), ()))


def kernel(
    counts_hbm,
    patches,
    in_w_hbm,
    out_w_hbm,
    gain1,
    shift1,
    in_bias,
    out_bias,
    gain2,
    shift2,
    mw_hbm,
    mbias_hbm,
    out,
    slot0,
    slot1,
    xbuf,
    hbuf,
    in_w,
    out_w,
    vec,
    vec2,
    in_b,
    vt,
    vt2,
    vt3,
    mw,
    mbias,
    normed,
    proj,
    stat,
    resid,
    wbuf,
    merged,
    pbuf,
    xpb,
    rel_a,
    rel_b,
    rs_a,
    rs_b,
    fa1,
    fa2,
    fb1,
    fb2,
    last,
    obuf,
    counts,
    local_sem,
    out_sem,
    part_send,
    part_recv,
    g_send,
    g_recv,
    h_send,
    h_recv,
    st_send,
    st_recv,
    ya_send,
    ya_recv,
    yb_send,
    yb_recv,
    za_send,
    za_recv,
    zb_send,
    zb_recv,
    pf_send,
    pf_recv,
    rs_send,
    rs_recv,
    last_send,
    last_recv,
):
    rank = lax.axis_index("dp")
    t = lax.axis_index("tensor")
    c = lax.rem(rank, 2)
    y = lax.rem(rank // 2, NY)
    z = rank // (2 * NY)
    partner = rank + 1 - 2 * c
    right = lax.rem(t + 1, NX)
    left = lax.rem(t + NX - 1, NX)
    across = lax.rem(t + 2, NX)

    def zwrap(k):
        return lax.rem(k + NZ, NZ)

    def rank_of(zz, yy):
        return (zz * NY + yy) * 2 + c

    up = rank_of(zwrap(z + 1), y)
    down = rank_of(zwrap(z - 1), y)

    peers = [(rank, right), (rank, left), (partner, right), (partner, left), (rank, across), (partner, across), (partner, t)]
    peers += [(rank_of(z, lax.rem(y + dy, NY)), t) for dy in range(1, NY)]
    peers += [(up, t), (down, t)]
    barrier = pltpu.get_barrier_semaphore()
    for peer in peers:
        pl.semaphore_signal(barrier, inc=1, device_id=peer, device_id_type=MESH)

    def load(src, dst, index):
        copy = pltpu.make_async_copy(src, dst, local_sem.at[index])
        copy.start()
        return copy

    mw_copy = load(mw_hbm, mw, 0)
    first = load(patches.at[:, pl.ds(0, TILE)], slot0, 1)
    counted = load(counts_hbm, counts, 15)
    small = [load(gain1, vec.at[0], 2), load(shift1, vec.at[1], 3)]
    small += [load(in_bias, in_b, 4)]
    small += [load(out_bias, vec2.at[3], 7), load(gain2, vec2.at[4], 8)]
    small += [load(shift2, vec2.at[5], 9), load(mbias_hbm, mbias.at[0], 10)]
    win_copies = [load(in_w_hbm.at[k], in_w.at[:, k], 11 + k) for k in range(3)]
    wout_copy = load(out_w_hbm, out_w, 14)
    pl.semaphore_wait(barrier, len(peers))

    def remote(src, dst, send, recv, device):
        return pltpu.make_async_remote_copy(
            src_ref=src, dst_ref=dst, send_sem=send, recv_sem=recv, device_id=device, device_id_type=MESH
        )

    def send(*args):
        copy = remote(*args)
        copy.start()

    def piece(i):
        return pl.ds(i * HEAD, HEAD)

    swaps = [
        remote(patches.at[piece(i), pl.ds(TILE, TILE)], slot1.at[piece(i)], part_send.at[i], part_recv.at[i], (partner, t))
        for i in range(LOCAL_HEADS)
    ]
    for i in (0, 1, 2, 3):
        swaps[i].start()
    mw_copy.wait()
    wbuf[z, y, c] = jnp.concatenate([mw[j] for j in range(4)], axis=1)
    for copy in small:
        copy.wait()
    vt[...] = jnp.transpose(vec[...])
    vt2[...] = jnp.transpose(vec2[...])
    vt3[...] = jnp.transpose(jnp.concatenate([in_b[...], jnp.zeros((5, BLOCK), F32)], axis=0))

    def sub(buf, owner, h):
        return buf.at[pl.ds(pl.multiple_of(owner * BLOCK + h * HEAD, 16), HEAD)]

    def gather_copy(buf, send, recv, owner, h, way, hop):
        ref = sub(buf, owner, h)
        return remote(ref, ref, send, recv.at[way, hop, h], (rank, right if way == 0 else left))

    def gather_wait(buf, send, recv, h, way, hop):
        owner = lax.rem(t + (NX - 1 - hop if way == 0 else 1 + hop), NX)
        ref = sub(buf, owner, h)
        remote(ref, ref, send, recv.at[way, hop, h], (rank, right)).wait_recv()

    def own_send(buf, send, recv, h, way):
        copy = gather_copy(buf, send, recv, t, h, way, 0)
        copy.start()

    def forward(buf, send, recv, h):
        way = h % 2
        gather_wait(buf, send, recv, h, way, 0)
        owner = left if way == 0 else right
        copy = gather_copy(buf, send, recv, owner, h, way, 1)
        copy.start()

    def near_wait(buf, send, recv):
        for h in range(LOCAL_HEADS):
            gather_wait(buf, send, recv, h, 1 - h % 2, 0)

    def far_wait(buf, send, recv):
        for h in range(LOCAL_HEADS):
            gather_wait(buf, send, recv, h, h % 2, 1)

    half_a, half_b = pl.ds(0, SPLIT), pl.ds(SPLIT, D - SPLIT)

    def arrived(ref, recv):
        remote(ref, ref, g_send, recv, (partner, t)).wait_recv()

    def z_origin(way, k):
        return zwrap(z - k) if way == 0 else zwrap(z + k)

    def z_send_a(way, k):
        if k <= PHASES - way:
            ref = wbuf.at[z_origin(way, k - 1), :, c, :, half_a]
            send(ref, ref, za_send, za_recv.at[way, k - 1], ((up, down)[way], t))

    def z_send_b(way, k):
        if k <= PHASES - way:
            ref = wbuf.at[z_origin(way, k - 1), y, c, :, half_b]
            send(ref, ref, zb_send, zb_recv.at[way, k - 1], ((up, down)[way], t))

    def blocks_of(k):
        if k == 0:
            return ((0, z),)
        if k == PHASES:
            return ((2 * PHASES - 1, zwrap(z - PHASES)),)
        return ((2 * k - 1, zwrap(z - k)), (2 * k, zwrap(z + k)))

    def y_block(zz, dy):
        return wbuf.at[zz, lax.rem(y + NY - dy, NY), c, :, half_b]

    def y_peer(dy):
        return (rank_of(z, lax.rem(y + dy, NY)), t)

    def y_send_b(k):
        for index, zz in blocks_of(k):
            ref = y_block(zz, 0)
            for dy in (1, 3, 2):
                send(ref, ref, yb_send, yb_recv.at[index, dy - 1], y_peer(dy))

    def hand_over(k):
        for index, zz in blocks_of(k):
            for dy in (1, 3, 2):
                arrived(y_block(zz, dy), yb_recv.at[index, dy - 1])
            ref = wbuf.at[zz, :, c]
            send(ref, ref, pf_send, pf_recv.at[index], (partner, t))

    def hand_wait(k):
        for index, zz in blocks_of(k):
            arrived(wbuf.at[zz, :, 1 - c], pf_recv.at[index])

    def weights_begin():
        ref = wbuf.at[z, y, c, :, half_a]
        for dy in (1, 3, 2):
            send(ref, ref, ya_send, ya_recv.at[dy - 1], (rank_of(z, lax.rem(y + dy, NY)), t))
        z_send_b(0, 1)
        z_send_b(1, 1)
        y_send_b(0)

    def weights_first():
        for dy in range(1, NY):
            arrived(wbuf.at[z, lax.rem(y + NY - dy, NY), c, :, half_a], ya_recv.at[dy - 1])
        z_send_a(0, 1)
        z_send_a(1, 1)

    def weights_step(k):
        if k == 0:
            weights_first()
            return
        if k <= PHASES:
            for way, (index, zz) in enumerate(blocks_of(k)):
                arrived(wbuf.at[zz, :, c, :, half_a], za_recv.at[way, k - 1])
                z_send_a(way, k + 1)
            for way, (index, zz) in enumerate(blocks_of(k)):
                arrived(wbuf.at[zz, y, c, :, half_b], zb_recv.at[way, k - 1])
                z_send_b(way, k + 1)
        if k <= PHASES:
            y_send_b(k)
        hand_over(k - 1)

    counted.wait()
    own0 = counts[2 * rank]
    other1 = counts[2 * partner + 1]
    tile_count = jnp.where(own0 > 0, own0, other1)
    first.wait()
    weights_begin()
    own_live = jnp.full((HEAD, TILE), own0, jnp.int32) > 0

    def choose(i):
        swaps[i].wait_recv()
        value = jnp.where(own_live, slot0[piece(i), :].astype(F32), slot1[piece(i), :].astype(F32))
        xbuf[pl.ds(pl.multiple_of(t * BLOCK + i * HEAD, 16), HEAD), :] = value.astype(BF16)

    for i in range(LOCAL_HEADS):
        choose(i)
    for h in (0, 2, 1, 3):
        own_send(xbuf, g_send, g_recv, h, 0)
        own_send(xbuf, g_send, g_recv, (h + 1) if h % 2 == 0 else (h - 1), 1)
    weights_step(0)

    def block_stats(owner):
        base = owner * BLOCK

        def total_of(i, acc):
            x = xbuf[pl.ds(pl.multiple_of(base + i * CHUNK, 16), CHUNK), :].astype(F32)
            return acc + jnp.sum(x, axis=0, keepdims=True)

        centre = lax.fori_loop(0, BLOCK // CHUNK, total_of, zero_row) * (1.0 / BLOCK)

        def spread_of(i, acc):
            x = xbuf[pl.ds(pl.multiple_of(base + i * CHUNK, 16), CHUNK), :].astype(F32) - centre
            return acc + jnp.sum(x * x, axis=0, keepdims=True)

        return centre, lax.fori_loop(0, BLOCK // CHUNK, spread_of, zero_row)

    zero_row = jnp.zeros((1, TILE), F32)
    stats = [block_stats(t)]
    for h in range(LOCAL_HEADS):
        forward(xbuf, g_send, g_recv, h)
    weights_step(1)
    near_wait(xbuf, g_send, g_recv)
    stats += [block_stats(left), block_stats(right)]
    weights_step(2)
    far_wait(xbuf, g_send, g_recv)
    stats += [block_stats(across)]
    mean = (stats[0][0] + stats[1][0] + stats[2][0] + stats[3][0]) * (1.0 / NX)
    spread = zero_row
    for centre, squares in stats:
        off = centre - mean
        spread = spread + squares + float(BLOCK) * (off * off)
    inv = lax.rsqrt(spread * (1.0 / D) + EPS)

    def normalise(i, carry):
        rows = pl.ds(pl.multiple_of(i * CHUNK, 16), CHUNK)
        x = xbuf[rows, :].astype(F32)
        gain = vt[rows, 0:1]
        shift = vt[rows, 1:2]
        normed[rows, :] = ((x - mean) * inv * gain + shift).astype(BF16)
        return carry

    lax.fori_loop(0, D // CHUNK, normalise, 0)

    for copy in win_copies:
        copy.wait()
    scale = 1.0 / math.sqrt(HEAD)

    def attend(h):
        got = jnp.dot(in_w[h].reshape(3 * HEAD, D), normed[...], preferred_element_type=F32)
        bias = jnp.concatenate([vt3[h * HEAD : (h + 1) * HEAD, k : k + 1] for k in range(3)], axis=0)
        proj[0 : 3 * HEAD, :] = (got + bias).astype(BF16)
        live = lax.broadcasted_iota(jnp.int32, (TILE, TILE // 2), 0) < tile_count

        def columns(i, carry):
            cols = pl.ds(pl.multiple_of(i * (TILE // 2), 128), TILE // 2)
            scores = lax.dot_general(
                proj[HEAD : 2 * HEAD, :], proj[0:HEAD, cols], TN, preferred_element_type=F32
            )
            scores = jnp.where(live, scores * scale, MASKED)
            highest = jnp.max(scores, axis=0, keepdims=True)
            raised = jnp.exp(scores - highest)
            weights = (raised * (1.0 / jnp.sum(raised, axis=0, keepdims=True))).astype(BF16)
            got = jnp.dot(proj[2 * HEAD : 3 * HEAD, :], weights, preferred_element_type=F32)
            hbuf[pl.ds(pl.multiple_of(t * BLOCK + h * HEAD, 16), HEAD), cols] = got.astype(BF16)
            return carry

        lax.fori_loop(0, 2, columns, 0)

    for h in range(LOCAL_HEADS):
        attend(h)
        own_send(hbuf, h_send, h_recv, h, 0)
        own_send(hbuf, h_send, h_recv, h, 1)
        if h == 1:
            weights_step(3)
        if h >= 2:
            forward(hbuf, h_send, h_recv, h - 2)
    weights_step(4)
    forward(hbuf, h_send, h_recv, 2)
    forward(hbuf, h_send, h_recv, 3)
    near_wait(hbuf, h_send, h_recv)
    weights_step(5)
    far_wait(hbuf, h_send, h_recv)

    wout_copy.wait()
    got = jnp.dot(out_w[...], hbuf[...], preferred_element_type=F32)
    resid[...] = xbuf[pl.ds(pl.multiple_of(t * BLOCK, 16), BLOCK), :].astype(F32) + got + vt2[:, 3:4]

    def sums_of(i, acc):
        x = resid[pl.ds(pl.multiple_of(i * CHUNK, 16), CHUNK), :]
        return acc[0] + jnp.sum(x, axis=0, keepdims=True), acc[1] + jnp.sum(x * x, axis=0, keepdims=True)

    row_sum, row_squares = lax.fori_loop(0, BLOCK // CHUNK, sums_of, (zero_row, zero_row))
    stat[3] = jnp.concatenate([row_sum, row_squares, jnp.zeros((6, TILE), F32)], axis=0)
    targets = (right, left, across)
    for k in range(3):
        send(stat.at[3], stat.at[k], st_send, st_recv.at[k], (rank, targets[k]))
    weights_step(6)
    for k in range(3):
        arrived(stat.at[k], st_recv.at[k])
    sums = stat[0] + stat[1] + stat[2] + stat[3]
    row_mean = sums[0:1] * (1.0 / D)
    second = sums[1:2] * (1.0 / D)
    inv2 = lax.rsqrt(second - row_mean * row_mean + EPS)

    def encode(i, carry):
        rows = pl.ds(pl.multiple_of(i * CHUNK, 16), CHUNK)
        x = resid[rows, :]
        value = (x - row_mean) * inv2 * vt2[rows, 4:5] + vt2[rows, 5:6]
        proj[rows, :] = value.astype(BF16)
        return carry

    lax.fori_loop(0, BLOCK // CHUNK, encode, 0)
    pieces = []
    for j in range(4):
        chosen = (
            lax.broadcasted_iota(jnp.int32, (MROWS, TILE), 1)
            == 4 * lax.broadcasted_iota(jnp.int32, (MROWS, TILE), 0) + j
        )
        pick = jnp.where(chosen, 1.0, 0.0).astype(BF16)
        pieces.append(lax.dot_general(pick, proj[0:BLOCK, :], NT, preferred_element_type=F32))
    merged[...] = jnp.concatenate(pieces, axis=1).astype(BF16)

    same = pl.multiple_of(lax.rem(t, 2) * HALF, 16)
    other = pl.multiple_of(HALF - lax.rem(t, 2) * HALF, 16)
    upper = t // 2
    right_up, left_up = right // 2, left // 2
    right_rank = rank + (partner - rank) * right_up
    left_rank = rank + (partner - rank) * left_up
    across_rank = rank + (partner - rank) * (across // 2)

    def rs_copies(s):
        a_same, b_same = pl.ds(same, QUARTER), pl.ds(pl.multiple_of(same + QUARTER, 16), QUARTER)
        a_other, b_other = pl.ds(other, QUARTER), pl.ds(pl.multiple_of(other + QUARTER, 16), QUARTER)
        return (
            remote(pbuf.at[s, a_same], rel_a.at[s], rs_send.at[0], rs_recv.at[s, 0], (rank, right)),
            remote(pbuf.at[s, b_same], rel_b.at[s], rs_send.at[1], rs_recv.at[s, 1], (rank, left)),
            remote(pbuf.at[s, b_other], fb1.at[s], rs_send.at[2], rs_recv.at[s, 2], (right_rank, right)),
            remote(pbuf.at[s, a_other], fa1.at[s], rs_send.at[3], rs_recv.at[s, 3], (left_rank, left)),
            remote(rs_a.at[s], fa2.at[s], rs_send.at[4], rs_recv.at[s, 4], (right_rank, right)),
            remote(rs_b.at[s], fb2.at[s], rs_send.at[5], rs_recv.at[s, 5], (left_rank, left)),
            remote(pbuf.at[s, pl.ds(same, HALF)], xpb.at[s], rs_send.at[6], rs_recv.at[s, 6], (partner, t)),
        )

    def z_of(s):
        return (zwrap(z - s), zwrap(z + s)) if s else (z, zwrap(z - PHASES))

    def project_block(s, k):
        part = wbuf[z_of(s)[k]].reshape(ZCOLS, D)
        got = lax.dot_general(merged[...], part, NT, preferred_element_type=F32)
        pbuf[s, :, k * ZCOLS : (k + 1) * ZCOLS] = got.astype(BF16)

    def project(s):
        project_block(s, 0)
        project_block(s, 1)
        copies = rs_copies(s)
        for k in (0, 1, 6):
            copies[k].start()

    def straight(k):
        mine_rows, their_rows, cols = pl.ds(same, HALF), pl.ds(other, HALF), pl.ds(k * ZCOLS, ZCOLS)
        return tuple(
            remote(pbuf.at[0, rows, cols], last.at[i, :, cols], last_send, last_recv.at[k, i], device)
            for i, (rows, device) in enumerate(
                (
                    (mine_rows, (across_rank, across)),
                    (their_rows, (right_rank, right)),
                    (their_rows, (left_rank, left)),
                    (mine_rows, (partner, t)),
                )
            )
        )

    def straight_phase(k):
        hand_wait(k * PHASES)
        project_block(0, k)
        for copy in straight(k):
            copy.start()

    def direct(s):
        copies = rs_copies(s)
        for k in (2, 3):
            copies[k].start()

    def relay(s):
        copies = rs_copies(s)
        copies[0].wait_recv()
        own = pbuf[s, pl.ds(other, QUARTER), :].astype(F32)
        rs_a[s] = (rel_a[s].astype(F32) + own).astype(BF16)
        copies[4].start()
        copies[1].wait_recv()
        own = pbuf[s, pl.ds(pl.multiple_of(other + QUARTER, 16), QUARTER), :].astype(F32)
        rs_b[s] = (rel_b[s].astype(F32) + own).astype(BF16)
        copies[5].start()

    my_count = counts[2 * rank + upper]
    written = []

    def collect(s):
        copies = rs_copies(s)
        if s:
            for k in (2, 3, 4, 5, 6):
                copies[k].wait_recv()
        else:
            for copy in straight(0) + straight(1):
                copy.wait_recv()
        local = pbuf[s, pl.ds(same, HALF), :].astype(F32)
        passed = (xpb[s] if s else last[3]).astype(F32)
        is_upper = jnp.full((HALF, 2 * ZCOLS), upper, jnp.int32) > 0
        total = jnp.where(is_upper, passed, local)
        if s == 0:
            total = total + last[0].astype(F32) + last[1].astype(F32) + last[2].astype(F32)
        else:
            top = fa1[s].astype(F32) + fa2[s].astype(F32)
            bottom = fb1[s].astype(F32) + fb2[s].astype(F32)
            total = total + jnp.concatenate([top, bottom], axis=0)
        row = lax.broadcasted_iota(jnp.int32, (HALF, ZCOLS), 0) + lax.rem(t, 2) * HALF
        keep = 4 * row < my_count
        for k, zz in enumerate(z_of(s)):
            cols = pl.ds(pl.multiple_of(zz * ZCOLS, 128), ZCOLS)
            value = total[:, k * ZCOLS : (k + 1) * ZCOLS] + mbias[:, cols]
            obuf[:, cols] = jnp.where(keep, value, 0.0).astype(BF16)
            copy = pltpu.make_async_copy(obuf.at[:, cols], out.at[:, cols], out_sem.at[s, k])
            copy.start()
            written.append(copy)

    def phase(s):
        hand_wait(s)
        project(s)

    for s in (1, 2, 3, 4):
        phase(s)
    straight_phase(0)
    weights_step(7)
    phase(5)
    for s in (1, 2, 3):
        relay(s)
        direct(s)
    phase(6)
    relay(4)
    direct(4)
    weights_step(8)
    relay(5)
    direct(5)
    phase(7)
    direct(6)
    for s in (1, 2, 3):
        collect(s)
    relay(6)
    direct(7)
    collect(4)
    weights_step(9)
    relay(7)
    collect(5)
    straight_phase(1)
    for s in (6, 7, 0):
        collect(s)

    def all_left(ref, sem):
        remote(ref, ref, sem, part_recv.at[0], (partner, t)).wait_send()

    for copy in swaps:
        copy.wait_send()
    all_left(xbuf.at[pl.ds(0, 3 * BLOCK)], g_send)
    all_left(hbuf.at[pl.ds(0, 3 * BLOCK)], h_send)
    all_left(stat.at[pl.ds(0, 3)], st_send)
    all_left(wbuf.at[pl.ds(0, NY - 1), y, c, :, half_a], ya_send)
    all_left(wbuf.at[pl.ds(0, 3 * NZ // 4), :, c, :, half_b], yb_send)
    all_left(wbuf.at[pl.ds(0, NZ - 1), :, c, :, half_a], za_send)
    all_left(wbuf.at[pl.ds(0, NZ - 1), y, c, :, half_b], zb_send)
    all_left(wbuf.at[:, :, c], pf_send)
    for k in range(6):
        all_left(rel_a.at[pl.ds(0, PHASES - 1)], rs_send.at[k])
    all_left(xpb.at[pl.ds(0, 4)], last_send)
    all_left(xpb.at[pl.ds(0, PHASES - 1)], rs_send.at[6])
    for copy in written:
        copy.wait()


def per_device(
    patches,
    counts,
    first_gain,
    first_shift,
    in_weight,
    in_bias,
    out_weight,
    out_bias,
    second_gain,
    second_shift,
    merger_weight,
    merger_bias,
):
    any_spec = pl.BlockSpec(memory_space=pl.ANY)
    dma = pltpu.SemaphoreType.DMA
    return pl.pallas_call(
        kernel,
        out_shape=jax.ShapeDtypeStruct((HALF, LLMW), BF16),
        in_specs=[any_spec] * 12,
        out_specs=any_spec,
        scratch_shapes=[
            pltpu.VMEM((BLOCK, TILE), BF16),
            pltpu.VMEM((BLOCK, TILE), BF16),
            pltpu.VMEM((D, TILE), BF16),
            pltpu.VMEM((D, TILE), BF16),
            pltpu.VMEM((LOCAL_HEADS, 3, HEAD, D), BF16),
            pltpu.VMEM((BLOCK, D), BF16),
            pltpu.VMEM((8, D), F32),
            pltpu.VMEM((8, BLOCK), F32),
            pltpu.VMEM((3, BLOCK), F32),
            pltpu.VMEM((D, 8), F32),
            pltpu.VMEM((BLOCK, 8), F32),
            pltpu.VMEM((BLOCK, 8), F32),
            pltpu.VMEM((4, LLMW // 128, BLOCK), BF16),
            pltpu.VMEM((1, LLMW), F32),
            pltpu.VMEM((D, TILE), BF16),
            pltpu.VMEM((3 * BLOCK, TILE), BF16),
            pltpu.VMEM((4, 8, TILE), F32),
            pltpu.VMEM((BLOCK, TILE), F32),
            pltpu.VMEM((NZ, NY, 2, 32, D), BF16),
            pltpu.VMEM((MROWS, D), BF16),
            pltpu.VMEM((PHASES, MROWS, 2 * ZCOLS), BF16),
            pltpu.VMEM((PHASES, HALF, 2 * ZCOLS), BF16),
        ]
        + [pltpu.VMEM((PHASES, QUARTER, 2 * ZCOLS), BF16)] * 8
        + [pltpu.VMEM((4, HALF, 2 * ZCOLS), BF16)]
        + [pltpu.VMEM((HALF, LLMW), BF16)]
        + [pltpu.SMEM((256,), jnp.int32)]
        + [dma((16,)), dma((PHASES, 2)), dma((LOCAL_HEADS,)), dma((LOCAL_HEADS,))]
        + [dma, dma((2, 2, LOCAL_HEADS))] * 2
        + [dma, dma((3,))]
        + [dma, dma((3,))]
        + [dma, dma((NZ, 3))]
        + [dma, dma((2, PHASES))] * 2
        + [dma, dma((NZ,)), dma((7,)), dma((PHASES, 7)), dma, dma((2, 4))],
        compiler_params=pltpu.CompilerParams(
            collective_id=0, has_side_effects=True, vmem_limit_bytes=60 * 1024 * 1024
        ),
        name="vision_block",
    )(
        counts,
        patches.T,
        jnp.transpose(in_weight, (1, 2, 0)).reshape(3, LOCAL_HEADS, HEAD, D),
        out_weight.T,
        first_gain,
        first_shift,
        in_bias,
        out_bias,
        second_gain,
        second_shift,
        jnp.transpose(merger_weight, (0, 2, 1)),
        merger_bias,
    )


def solution(mesh):
    return jax.shard_map(
        per_device,
        mesh=mesh,
        in_specs=(
            P("dp", "tensor"),
            P(),
            P(),
            P(),
            P(None, None, "tensor"),
            P(None, "tensor"),
            P(None, "tensor"),
            P("tensor"),
            P("tensor"),
            P("tensor"),
            P(None, "tensor", "dp"),
            P(),
        ),
        out_specs=P(("dp", "tensor"), None),
        check_vma=False,
    )
```

```python
import functools
import math

import jax
import jax.numpy as jnp
from jax import lax
from jax.experimental import pallas as pl
from jax.experimental.pallas import tpu as pltpu
from jax.sharding import PartitionSpec as P

D = 1280
HEADS = 16
TILE = 512
NX = 4
NY = 4
NZ = 16
BLOCK = D // NX
HEAD = D // HEADS
LOCAL_HEADS = BLOCK // HEAD
LLMW = 4096
MROWS = TILE // 4
HALF = MROWS // 2
QUARTER = HALF // 2
ZCOLS = LLMW // NZ
PHASES = NZ // 2

EPS = 1e-06
MASKED = -1e30
MESH = pl.DeviceIdType.MESH
F32 = jnp.float32
BF16 = jnp.bfloat16
CHUNK = 80
SPLIT = 512

NT = (((1,), (1,)), ((), ()))
TN = (((0,), (0,)), ((), ()))


def kernel(
    counts_hbm,
    patches,
    in_w_hbm,
    out_w_hbm,
    gain1,
    shift1,
    in_bias,
    out_bias,
    gain2,
    shift2,
    mw_hbm,
    mbias_hbm,
    out,
    slot0,
    slot1,
    xbuf,
    hbuf,
    in_w,
    out_w,
    vec,
    vec2,
    in_b,
    vt,
    vt2,
    vt3,
    mw,
    mbias,
    normed,
    proj,
    stat,
    resid,
    wbuf,
    merged,
    pbuf,
    xpb,
    rel_a,
    rel_b,
    rs_a,
    rs_b,
    fa1,
    fa2,
    fb1,
    fb2,
    last,
    obuf,
    counts,
    local_sem,
    out_sem,
    part_send,
    part_recv,
    g_send,
    g_recv,
    h_send,
    h_recv,
    st_send,
    st_recv,
    ya_send,
    ya_recv,
    yb_send,
    yb_recv,
    za_send,
    za_recv,
    zb_send,
    zb_recv,
    pf_send,
    pf_recv,
    rs_send,
    rs_recv,
    last_send,
    last_recv,
):
    rank = lax.axis_index("dp")
    t = lax.axis_index("tensor")
    c = lax.rem(rank, 2)
    y = lax.rem(rank // 2, NY)
    z = rank // (2 * NY)
    partner = rank + 1 - 2 * c
    right = lax.rem(t + 1, NX)
    left = lax.rem(t + NX - 1, NX)
    across = lax.rem(t + 2, NX)

    def zwrap(k):
        return lax.rem(k + NZ, NZ)

    def rank_of(zz, yy):
        return (zz * NY + yy) * 2 + c

    up = rank_of(zwrap(z + 1), y)
    down = rank_of(zwrap(z - 1), y)

    peers = [(rank, right), (rank, left), (partner, right), (partner, left), (rank, across), (partner, across), (partner, t)]
    peers += [(rank_of(z, lax.rem(y + dy, NY)), t) for dy in range(1, NY)]
    peers += [(up, t), (down, t)]
    barrier = pltpu.get_barrier_semaphore()
    for peer in peers:
        pl.semaphore_signal(barrier, inc=1, device_id=peer, device_id_type=MESH)

    def load(src, dst, index):
        copy = pltpu.make_async_copy(src, dst, local_sem.at[index])
        copy.start()
        return copy

    mw_copy = load(mw_hbm, mw, 0)
    first = load(patches.at[:, pl.ds(0, TILE)], slot0, 1)
    counted = load(counts_hbm, counts, 15)
    small = [load(gain1, vec.at[0], 2), load(shift1, vec.at[1], 3)]
    small += [load(in_bias, in_b, 4)]
    small += [load(out_bias, vec2.at[3], 7), load(gain2, vec2.at[4], 8)]
    small += [load(shift2, vec2.at[5], 9), load(mbias_hbm, mbias.at[0], 10)]
    win_copies = [load(in_w_hbm.at[k], in_w.at[:, k], 11 + k) for k in range(3)]
    wout_copy = load(out_w_hbm, out_w, 14)
    pl.semaphore_wait(barrier, len(peers))

    def remote(src, dst, send, recv, device):
        return pltpu.make_async_remote_copy(
            src_ref=src, dst_ref=dst, send_sem=send, recv_sem=recv, device_id=device, device_id_type=MESH
        )

    def send(*args):
        copy = remote(*args)
        copy.start()

    def piece(i):
        return pl.ds(i * HEAD, HEAD)

    swaps = [
        remote(patches.at[piece(i), pl.ds(TILE, TILE)], slot1.at[piece(i)], part_send.at[i], part_recv.at[i], (partner, t))
        for i in range(LOCAL_HEADS)
    ]
    for i in (0, 1, 2, 3):
        swaps[i].start()
    mw_copy.wait()
    wbuf[z, y, c] = jnp.concatenate([mw[j] for j in range(4)], axis=1)
    for copy in small:
        copy.wait()
    vt[...] = jnp.transpose(vec[...])
    vt2[...] = jnp.transpose(vec2[...])
    vt3[...] = jnp.transpose(jnp.concatenate([in_b[...], jnp.zeros((5, BLOCK), F32)], axis=0))

    def sub(buf, owner, h):
        return buf.at[pl.ds(pl.multiple_of(owner * BLOCK + h * HEAD, 16), HEAD)]

    def gather_copy(buf, send, recv, owner, h, way, hop):
        ref = sub(buf, owner, h)
        return remote(ref, ref, send, recv.at[way, hop, h], (rank, right if way == 0 else left))

    def gather_wait(buf, send, recv, h, way, hop):
        owner = lax.rem(t + (NX - 1 - hop if way == 0 else 1 + hop), NX)
        ref = sub(buf, owner, h)
        remote(ref, ref, send, recv.at[way, hop, h], (rank, right)).wait_recv()

    def own_send(buf, send, recv, h, way):
        copy = gather_copy(buf, send, recv, t, h, way, 0)
        copy.start()

    def forward(buf, send, recv, h):
        way = h % 2
        gather_wait(buf, send, recv, h, way, 0)
        owner = left if way == 0 else right
        copy = gather_copy(buf, send, recv, owner, h, way, 1)
        copy.start()

    def near_wait(buf, send, recv):
        for h in range(LOCAL_HEADS):
            gather_wait(buf, send, recv, h, 1 - h % 2, 0)

    def far_wait(buf, send, recv):
        for h in range(LOCAL_HEADS):
            gather_wait(buf, send, recv, h, h % 2, 1)

    half_a, half_b = pl.ds(0, SPLIT), pl.ds(SPLIT, D - SPLIT)

    def arrived(ref, recv):
        remote(ref, ref, g_send, recv, (partner, t)).wait_recv()

    def z_origin(way, k):
        return zwrap(z - k) if way == 0 else zwrap(z + k)

    def z_send_a(way, k):
        if k <= PHASES - way:
            ref = wbuf.at[z_origin(way, k - 1), :, c, :, half_a]
            send(ref, ref, za_send, za_recv.at[way, k - 1], ((up, down)[way], t))

    def z_send_b(way, k):
        if k <= PHASES - way:
            ref = wbuf.at[z_origin(way, k - 1), y, c, :, half_b]
            send(ref, ref, zb_send, zb_recv.at[way, k - 1], ((up, down)[way], t))

    def blocks_of(k):
        if k == 0:
            return ((0, z),)
        if k == PHASES:
            return ((2 * PHASES - 1, zwrap(z - PHASES)),)
        return ((2 * k - 1, zwrap(z - k)), (2 * k, zwrap(z + k)))

    def y_block(zz, dy):
        return wbuf.at[zz, lax.rem(y + NY - dy, NY), c, :, half_b]

    def y_peer(dy):
        return (rank_of(z, lax.rem(y + dy, NY)), t)

    def y_send_b(k):
        for index, zz in blocks_of(k):
            ref = y_block(zz, 0)
            for dy in (1, 3, 2):
                send(ref, ref, yb_send, yb_recv.at[index, dy - 1], y_peer(dy))

    def hand_over(k):
        for index, zz in blocks_of(k):
            for dy in (1, 3, 2):
                arrived(y_block(zz, dy), yb_recv.at[index, dy - 1])
            ref = wbuf.at[zz, :, c]
            send(ref, ref, pf_send, pf_recv.at[index], (partner, t))

    def hand_wait(k):
        for index, zz in blocks_of(k):
            arrived(wbuf.at[zz, :, 1 - c], pf_recv.at[index])

    def weights_begin():
        ref = wbuf.at[z, y, c, :, half_a]
        for dy in (1, 3, 2):
            send(ref, ref, ya_send, ya_recv.at[dy - 1], (rank_of(z, lax.rem(y + dy, NY)), t))
        z_send_b(0, 1)
        z_send_b(1, 1)
        y_send_b(0)

    def weights_first():
        for dy in range(1, NY):
            arrived(wbuf.at[z, lax.rem(y + NY - dy, NY), c, :, half_a], ya_recv.at[dy - 1])
        z_send_a(0, 1)
        z_send_a(1, 1)

    def weights_step(k):
        if k == 0:
            weights_first()
            return
        if k <= PHASES:
            for way, (index, zz) in enumerate(blocks_of(k)):
                arrived(wbuf.at[zz, :, c, :, half_a], za_recv.at[way, k - 1])
                z_send_a(way, k + 1)
            for way, (index, zz) in enumerate(blocks_of(k)):
                arrived(wbuf.at[zz, y, c, :, half_b], zb_recv.at[way, k - 1])
                z_send_b(way, k + 1)
        if k <= PHASES:
            y_send_b(k)
        hand_over(k - 1)

    counted.wait()
    own0 = counts[2 * rank]
    other1 = counts[2 * partner + 1]
    tile_count = jnp.where(own0 > 0, own0, other1)
    first.wait()
    weights_begin()
    own_live = jnp.full((HEAD, TILE), own0, jnp.int32) > 0

    def choose(i):
        swaps[i].wait_recv()
        value = jnp.where(own_live, slot0[piece(i), :].astype(F32), slot1[piece(i), :].astype(F32))
        xbuf[pl.ds(pl.multiple_of(t * BLOCK + i * HEAD, 16), HEAD), :] = value.astype(BF16)

    for i in range(LOCAL_HEADS):
        choose(i)
    for h in (0, 2, 1, 3):
        own_send(xbuf, g_send, g_recv, h, 0)
        own_send(xbuf, g_send, g_recv, (h + 1) if h % 2 == 0 else (h - 1), 1)
    weights_step(0)

    def block_stats(owner):
        base = owner * BLOCK

        def total_of(i, acc):
            x = xbuf[pl.ds(pl.multiple_of(base + i * CHUNK, 16), CHUNK), :].astype(F32)
            return acc + jnp.sum(x, axis=0, keepdims=True)

        centre = lax.fori_loop(0, BLOCK // CHUNK, total_of, zero_row) * (1.0 / BLOCK)

        def spread_of(i, acc):
            x = xbuf[pl.ds(pl.multiple_of(base + i * CHUNK, 16), CHUNK), :].astype(F32) - centre
            return acc + jnp.sum(x * x, axis=0, keepdims=True)

        return centre, lax.fori_loop(0, BLOCK // CHUNK, spread_of, zero_row)

    zero_row = jnp.zeros((1, TILE), F32)
    stats = [block_stats(t)]
    for h in range(LOCAL_HEADS):
        forward(xbuf, g_send, g_recv, h)
    weights_step(1)
    near_wait(xbuf, g_send, g_recv)
    stats += [block_stats(left), block_stats(right)]
    weights_step(2)
    far_wait(xbuf, g_send, g_recv)
    stats += [block_stats(across)]
    mean = (stats[0][0] + stats[1][0] + stats[2][0] + stats[3][0]) * (1.0 / NX)
    spread = zero_row
    for centre, squares in stats:
        off = centre - mean
        spread = spread + squares + float(BLOCK) * (off * off)
    inv = lax.rsqrt(spread * (1.0 / D) + EPS)

    def normalise(i, carry):
        rows = pl.ds(pl.multiple_of(i * CHUNK, 16), CHUNK)
        x = xbuf[rows, :].astype(F32)
        gain = vt[rows, 0:1]
        shift = vt[rows, 1:2]
        normed[rows, :] = ((x - mean) * inv * gain + shift).astype(BF16)
        return carry

    lax.fori_loop(0, D // CHUNK, normalise, 0)

    for copy in win_copies:
        copy.wait()
    scale = 1.0 / math.sqrt(HEAD)

    def attend(h):
        got = jnp.dot(in_w[h].reshape(3 * HEAD, D), normed[...], preferred_element_type=F32)
        bias = jnp.concatenate([vt3[h * HEAD : (h + 1) * HEAD, k : k + 1] for k in range(3)], axis=0)
        proj[0 : 3 * HEAD, :] = (got + bias).astype(BF16)
        live = lax.broadcasted_iota(jnp.int32, (TILE, TILE // 2), 0) < tile_count

        def columns(i, carry):
            cols = pl.ds(pl.multiple_of(i * (TILE // 2), 128), TILE // 2)
            scores = lax.dot_general(
                proj[HEAD : 2 * HEAD, :], proj[0:HEAD, cols], TN, preferred_element_type=F32
            )
            scores = jnp.where(live, scores * scale, MASKED)
            highest = jnp.max(scores, axis=0, keepdims=True)
            raised = jnp.exp(scores - highest)
            weights = (raised * (1.0 / jnp.sum(raised, axis=0, keepdims=True))).astype(BF16)
            got = jnp.dot(proj[2 * HEAD : 3 * HEAD, :], weights, preferred_element_type=F32)
            hbuf[pl.ds(pl.multiple_of(t * BLOCK + h * HEAD, 16), HEAD), cols] = got.astype(BF16)
            return carry

        lax.fori_loop(0, 2, columns, 0)

    for h in range(LOCAL_HEADS):
        attend(h)
        own_send(hbuf, h_send, h_recv, h, 0)
        own_send(hbuf, h_send, h_recv, h, 1)
        if h == 1:
            weights_step(3)
        if h >= 2:
            forward(hbuf, h_send, h_recv, h - 2)
    weights_step(4)
    forward(hbuf, h_send, h_recv, 2)
    forward(hbuf, h_send, h_recv, 3)
    near_wait(hbuf, h_send, h_recv)
    weights_step(5)
    far_wait(hbuf, h_send, h_recv)

    wout_copy.wait()
    got = jnp.dot(out_w[...], hbuf[...], preferred_element_type=F32)
    resid[...] = xbuf[pl.ds(pl.multiple_of(t * BLOCK, 16), BLOCK), :].astype(F32) + got + vt2[:, 3:4]

    def sums_of(i, acc):
        x = resid[pl.ds(pl.multiple_of(i * CHUNK, 16), CHUNK), :]
        return acc[0] + jnp.sum(x, axis=0, keepdims=True), acc[1] + jnp.sum(x * x, axis=0, keepdims=True)

    row_sum, row_squares = lax.fori_loop(0, BLOCK // CHUNK, sums_of, (zero_row, zero_row))
    stat[3] = jnp.concatenate([row_sum, row_squares, jnp.zeros((6, TILE), F32)], axis=0)
    targets = (right, left, across)
    for k in range(3):
        send(stat.at[3], stat.at[k], st_send, st_recv.at[k], (rank, targets[k]))
    for k in range(3):
        arrived(stat.at[k], st_recv.at[k])
    sums = stat[0] + stat[1] + stat[2] + stat[3]
    row_mean = sums[0:1] * (1.0 / D)
    second = sums[1:2] * (1.0 / D)
    inv2 = lax.rsqrt(second - row_mean * row_mean + EPS)

    def encode(i, carry):
        rows = pl.ds(pl.multiple_of(i * CHUNK, 16), CHUNK)
        x = resid[rows, :]
        value = (x - row_mean) * inv2 * vt2[rows, 4:5] + vt2[rows, 5:6]
        proj[rows, :] = value.astype(BF16)
        return carry

    lax.fori_loop(0, BLOCK // CHUNK, encode, 0)
    pieces = []
    for j in range(4):
        chosen = (
            lax.broadcasted_iota(jnp.int32, (MROWS, TILE), 1)
            == 4 * lax.broadcasted_iota(jnp.int32, (MROWS, TILE), 0) + j
        )
        pick = jnp.where(chosen, 1.0, 0.0).astype(BF16)
        pieces.append(lax.dot_general(pick, proj[0:BLOCK, :], NT, preferred_element_type=F32))
    merged[...] = jnp.concatenate(pieces, axis=1).astype(BF16)

    same = pl.multiple_of(lax.rem(t, 2) * HALF, 16)
    other = pl.multiple_of(HALF - lax.rem(t, 2) * HALF, 16)
    upper = t // 2
    right_up, left_up = right // 2, left // 2
    right_rank = rank + (partner - rank) * right_up
    left_rank = rank + (partner - rank) * left_up
    across_rank = rank + (partner - rank) * (across // 2)

    def rs_copies(s):
        a_same, b_same = pl.ds(same, QUARTER), pl.ds(pl.multiple_of(same + QUARTER, 16), QUARTER)
        a_other, b_other = pl.ds(other, QUARTER), pl.ds(pl.multiple_of(other + QUARTER, 16), QUARTER)
        return (
            remote(pbuf.at[s, a_same], rel_a.at[s], rs_send.at[0], rs_recv.at[s, 0], (rank, right)),
            remote(pbuf.at[s, b_same], rel_b.at[s], rs_send.at[1], rs_recv.at[s, 1], (rank, left)),
            remote(pbuf.at[s, b_other], fb1.at[s], rs_send.at[2], rs_recv.at[s, 2], (right_rank, right)),
            remote(pbuf.at[s, a_other], fa1.at[s], rs_send.at[3], rs_recv.at[s, 3], (left_rank, left)),
            remote(rs_a.at[s], fa2.at[s], rs_send.at[4], rs_recv.at[s, 4], (right_rank, right)),
            remote(rs_b.at[s], fb2.at[s], rs_send.at[5], rs_recv.at[s, 5], (left_rank, left)),
            remote(pbuf.at[s, pl.ds(same, HALF)], xpb.at[s], rs_send.at[6], rs_recv.at[s, 6], (partner, t)),
        )

    def z_of(s):
        return (zwrap(z - s), zwrap(z + s)) if s else (z, zwrap(z - PHASES))

    def project_block(s, k):
        part = wbuf[z_of(s)[k]].reshape(ZCOLS, D)
        got = lax.dot_general(merged[...], part, NT, preferred_element_type=F32)
        pbuf[s, :, k * ZCOLS : (k + 1) * ZCOLS] = got.astype(BF16)

    def project(s):
        project_block(s, 0)
        project_block(s, 1)
        copies = rs_copies(s)
        for k in (0, 1, 6):
            copies[k].start()

    def straight(k):
        mine_rows, their_rows, cols = pl.ds(same, HALF), pl.ds(other, HALF), pl.ds(k * ZCOLS, ZCOLS)
        return tuple(
            remote(pbuf.at[0, rows, cols], last.at[i, :, cols], last_send, last_recv.at[k, i], device)
            for i, (rows, device) in enumerate(
                (
                    (mine_rows, (across_rank, across)),
                    (their_rows, (right_rank, right)),
                    (their_rows, (left_rank, left)),
                    (mine_rows, (partner, t)),
                )
            )
        )

    def straight_phase(k):
        hand_wait(k * PHASES)
        project_block(0, k)
        for copy in straight(k):
            copy.start()

    def direct(s):
        copies = rs_copies(s)
        for k in (2, 3):
            copies[k].start()

    def relay(s):
        copies = rs_copies(s)
        copies[0].wait_recv()
        own = pbuf[s, pl.ds(other, QUARTER), :].astype(F32)
        rs_a[s] = (rel_a[s].astype(F32) + own).astype(BF16)
        copies[4].start()
        copies[1].wait_recv()
        own = pbuf[s, pl.ds(pl.multiple_of(other + QUARTER, 16), QUARTER), :].astype(F32)
        rs_b[s] = (rel_b[s].astype(F32) + own).astype(BF16)
        copies[5].start()

    my_count = counts[2 * rank + upper]
    written = []

    def collect(s):
        copies = rs_copies(s)
        if s:
            for k in (2, 3, 4, 5, 6):
                copies[k].wait_recv()
        else:
            for copy in straight(0) + straight(1):
                copy.wait_recv()
        local = pbuf[s, pl.ds(same, HALF), :].astype(F32)
        passed = (xpb[s] if s else last[3]).astype(F32)
        is_upper = jnp.full((HALF, 2 * ZCOLS), upper, jnp.int32) > 0
        total = jnp.where(is_upper, passed, local)
        if s == 0:
            total = total + last[0].astype(F32) + last[1].astype(F32) + last[2].astype(F32)
        else:
            top = fa1[s].astype(F32) + fa2[s].astype(F32)
            bottom = fb1[s].astype(F32) + fb2[s].astype(F32)
            total = total + jnp.concatenate([top, bottom], axis=0)
        row = lax.broadcasted_iota(jnp.int32, (HALF, ZCOLS), 0) + lax.rem(t, 2) * HALF
        keep = 4 * row < my_count
        for k, zz in enumerate(z_of(s)):
            cols = pl.ds(pl.multiple_of(zz * ZCOLS, 128), ZCOLS)
            value = total[:, k * ZCOLS : (k + 1) * ZCOLS] + mbias[:, cols]
            obuf[:, cols] = jnp.where(keep, value, 0.0).astype(BF16)
            copy = pltpu.make_async_copy(obuf.at[:, cols], out.at[:, cols], out_sem.at[s, k])
            copy.start()
            written.append(copy)

    def phase(s):
        hand_wait(s)
        project(s)

    phase(1)
    phase(2)
    weights_step(6)
    phase(3)
    phase(4)
    straight_phase(0)
    weights_step(7)
    phase(5)
    for s in (1, 2, 3):
        relay(s)
        direct(s)
    phase(6)
    relay(4)
    direct(4)
    weights_step(8)
    relay(5)
    direct(5)
    phase(7)
    direct(6)
    for s in (1, 2, 3):
        collect(s)
    relay(6)
    direct(7)
    collect(4)
    weights_step(9)
    relay(7)
    collect(5)
    straight_phase(1)
    for s in (6, 7, 0):
        collect(s)

    def all_left(ref, sem):
        remote(ref, ref, sem, part_recv.at[0], (partner, t)).wait_send()

    for copy in swaps:
        copy.wait_send()
    all_left(xbuf.at[pl.ds(0, 3 * BLOCK)], g_send)
    all_left(hbuf.at[pl.ds(0, 3 * BLOCK)], h_send)
    all_left(stat.at[pl.ds(0, 3)], st_send)
    all_left(wbuf.at[pl.ds(0, NY - 1), y, c, :, half_a], ya_send)
    all_left(wbuf.at[pl.ds(0, 3 * NZ // 4), :, c, :, half_b], yb_send)
    all_left(wbuf.at[pl.ds(0, NZ - 1), :, c, :, half_a], za_send)
    all_left(wbuf.at[pl.ds(0, NZ - 1), y, c, :, half_b], zb_send)
    all_left(wbuf.at[:, :, c], pf_send)
    for k in range(6):
        all_left(rel_a.at[pl.ds(0, PHASES - 1)], rs_send.at[k])
    all_left(xpb.at[pl.ds(0, 4)], last_send)
    all_left(xpb.at[pl.ds(0, PHASES - 1)], rs_send.at[6])
    for copy in written:
        copy.wait()


def per_device(
    patches,
    counts,
    first_gain,
    first_shift,
    in_weight,
    in_bias,
    out_weight,
    out_bias,
    second_gain,
    second_shift,
    merger_weight,
    merger_bias,
):
    any_spec = pl.BlockSpec(memory_space=pl.ANY)
    dma = pltpu.SemaphoreType.DMA
    return pl.pallas_call(
        kernel,
        out_shape=jax.ShapeDtypeStruct((HALF, LLMW), BF16),
        in_specs=[any_spec] * 12,
        out_specs=any_spec,
        scratch_shapes=[
            pltpu.VMEM((BLOCK, TILE), BF16),
            pltpu.VMEM((BLOCK, TILE), BF16),
            pltpu.VMEM((D, TILE), BF16),
            pltpu.VMEM((D, TILE), BF16),
            pltpu.VMEM((LOCAL_HEADS, 3, HEAD, D), BF16),
            pltpu.VMEM((BLOCK, D), BF16),
            pltpu.VMEM((8, D), F32),
            pltpu.VMEM((8, BLOCK), F32),
            pltpu.VMEM((3, BLOCK), F32),
            pltpu.VMEM((D, 8), F32),
            pltpu.VMEM((BLOCK, 8), F32),
            pltpu.VMEM((BLOCK, 8), F32),
            pltpu.VMEM((4, LLMW // 128, BLOCK), BF16),
            pltpu.VMEM((1, LLMW), F32),
            pltpu.VMEM((D, TILE), BF16),
            pltpu.VMEM((3 * BLOCK, TILE), BF16),
            pltpu.VMEM((4, 8, TILE), F32),
            pltpu.VMEM((BLOCK, TILE), F32),
            pltpu.VMEM((NZ, NY, 2, 32, D), BF16),
            pltpu.VMEM((MROWS, D), BF16),
            pltpu.VMEM((PHASES, MROWS, 2 * ZCOLS), BF16),
            pltpu.VMEM((PHASES, HALF, 2 * ZCOLS), BF16),
        ]
        + [pltpu.VMEM((PHASES, QUARTER, 2 * ZCOLS), BF16)] * 8
        + [pltpu.VMEM((4, HALF, 2 * ZCOLS), BF16)]
        + [pltpu.VMEM((HALF, LLMW), BF16)]
        + [pltpu.SMEM((256,), jnp.int32)]
        + [dma((16,)), dma((PHASES, 2)), dma((LOCAL_HEADS,)), dma((LOCAL_HEADS,))]
        + [dma, dma((2, 2, LOCAL_HEADS))] * 2
        + [dma, dma((3,))]
        + [dma, dma((3,))]
        + [dma, dma((NZ, 3))]
        + [dma, dma((2, PHASES))] * 2
        + [dma, dma((NZ,)), dma((7,)), dma((PHASES, 7)), dma, dma((2, 4))],
        compiler_params=pltpu.CompilerParams(
            collective_id=0, has_side_effects=True, vmem_limit_bytes=60 * 1024 * 1024
        ),
        name="vision_block",
    )(
        counts,
        patches.T,
        jnp.transpose(in_weight, (1, 2, 0)).reshape(3, LOCAL_HEADS, HEAD, D),
        out_weight.T,
        first_gain,
        first_shift,
        in_bias,
        out_bias,
        second_gain,
        second_shift,
        jnp.transpose(merger_weight, (0, 2, 1)),
        merger_bias,
    )


def solution(mesh):
    return jax.shard_map(
        per_device,
        mesh=mesh,
        in_specs=(
            P("dp", "tensor"),
            P(),
            P(),
            P(),
            P(None, None, "tensor"),
            P(None, "tensor"),
            P(None, "tensor"),
            P("tensor"),
            P("tensor"),
            P("tensor"),
            P(None, "tensor", "dp"),
            P(),
        ),
        out_specs=P(("dp", "tensor"), None),
        check_vma=False,
    )
```
